32 devices in a mesh: dp: 8 (over z, y), tensor: 4 (over x, core).
Axes of the slice: x: 2, y: 2, z: 4, core: 2. Of those that a mesh axis runs over, the one named last changes fastest.
Arguments:
- patches: bfloat16 [64, 196, 768], P('dp'), may hold values from -6 to 6
- cotangent: bfloat16 [64, 196, 768], P('dp'), may hold values from -6 to 6
- mask_rank: int32 [64, 196], P('dp'), may hold values from 0 to 195, each once within a row
- mask_count: int32 [64], P('dp'), may hold values from 78 to 156
- image_count: int32 [8], P('dp'), may hold values from 1 to 8, as said below
- entry_weight: float32 [3, 768, 768], P(None, 'dp', 'tensor'), may hold values from -0.21875 to 0.21875
- entry_moment: float32 [3, 768, 768], P(None, 'dp', 'tensor'), may hold values from -20 to 20
- entry_second: float32 [3, 768, 768], P(None, 'dp', 'tensor'), may hold values from 0.426496 to 6.77376
- entry_bias: float32 [2, 4, 192], P(None, 'tensor', 'dp'), may hold values from -4 to 4
- entry_bias_moment: float32 [2, 4, 192], P(None, 'tensor', 'dp'), may hold values from -20 to 20
- entry_bias_second: float32 [2, 4, 192], P(None, 'tensor', 'dp'), may hold values from 0.426496 to 6.77376
- exit_weight: float32 [768, 768], P('tensor', 'dp'), may hold values from -0.625 to 0.625
- exit_moment: float32 [768, 768], P('tensor', 'dp'), may hold values from -20 to 20
- exit_second: float32 [768, 768], P('tensor', 'dp'), may hold values from 0.426496 to 6.77376
- expand_weight: float32 [768, 3072], P('dp', 'tensor'), may hold values from -0.21875 to 0.21875
- expand_moment: float32 [768, 3072], P('dp', 'tensor'), may hold values from -20 to 20
- expand_second: float32 [768, 3072], P('dp', 'tensor'), may hold values from 0.426496 to 6.77376
- expand_bias: float32 [4, 768], P('tensor', 'dp'), may hold values from -4 to 4
- expand_bias_moment: float32 [4, 768], P('tensor', 'dp'), may hold values from -20 to 20
- expand_bias_second: float32 [4, 768], P('tensor', 'dp'), may hold values from 0.426496 to 6.77376
- reduce_weight: float32 [3072, 768], P('tensor', 'dp'), may hold values from -0.109375 to 0.109375
- reduce_moment: float32 [3072, 768], P('tensor', 'dp'), may hold values from -20 to 20
- reduce_second: float32 [3072, 768], P('tensor', 'dp'), may hold values from 0.426496 to 6.77376
- vectors: float32 [7, 768], P(None, 'dp'), may hold values from -6 to 6, as said below
- vectors_moment: float32 [7, 768], P(None, 'dp'), may hold values from -64 to 64
- vectors_second: float32 [7, 768], P(None, 'dp'), may hold values from 4.704 to 75.264
- position: float32 [196, 768], P(None, 'dp'), may hold values from -4 to 4
- position_moment: float32 [196, 768], P(None, 'dp'), may hold values from -4 to 4
- position_second: float32 [196, 768], P(None, 'dp'), may hold values from 0.064 to 0.512
Outputs:
- block_out: bfloat16 [64, 196, 768], P('dp')
- patch_grad: bfloat16 [64, 196, 768], P('dp')
- entry_new: float32 [3, 768, 768], P(None, 'dp', 'tensor')
- entry_moment_new: float32 [3, 768, 768], P(None, 'dp', 'tensor')
- entry_second_new: float32 [3, 768, 768], P(None, 'dp', 'tensor')
- entry_copy: bfloat16 [3, 768, 768], P(None, 'dp', 'tensor')
- entry_bias_new: float32 [2, 4, 192], P(None, 'tensor', 'dp')
- entry_bias_moment_new: float32 [2, 4, 192], P(None, 'tensor', 'dp')
- entry_bias_second_new: float32 [2, 4, 192], P(None, 'tensor', 'dp')
- entry_bias_copy: bfloat16 [2, 4, 192], P(None, 'tensor', 'dp')
- exit_new: float32 [768, 768], P('tensor', 'dp')
- exit_moment_new: float32 [768, 768], P('tensor', 'dp')
- exit_second_new: float32 [768, 768], P('tensor', 'dp')
- exit_copy: bfloat16 [768, 768], P('tensor', 'dp')
- expand_new: float32 [768, 3072], P('dp', 'tensor')
- expand_moment_new: float32 [768, 3072], P('dp', 'tensor')
- expand_second_new: float32 [768, 3072], P('dp', 'tensor')
- expand_copy: bfloat16 [768, 3072], P('dp', 'tensor')
- expand_bias_new: float32 [4, 768], P('tensor', 'dp')
- expand_bias_moment_new: float32 [4, 768], P('tensor', 'dp')
- expand_bias_second_new: float32 [4, 768], P('tensor', 'dp')
- expand_bias_copy: bfloat16 [4, 768], P('tensor', 'dp')
- reduce_new: float32 [3072, 768], P('tensor', 'dp')
- reduce_moment_new: float32 [3072, 768], P('tensor', 'dp')
- reduce_second_new: float32 [3072, 768], P('tensor', 'dp')
- reduce_copy: bfloat16 [3072, 768], P('tensor', 'dp')
- vectors_new: float32 [7, 768], P(None, 'dp')
- vectors_moment_new: float32 [7, 768], P(None, 'dp')
- vectors_second_new: float32 [7, 768], P(None, 'dp')
- vectors_copy: bfloat16 [7, 768], P(None, 'dp')
- position_new: float32 [196, 768], P(None, 'dp')
- position_moment_new: float32 [196, 768], P(None, 'dp')
- position_second_new: float32 [196, 768], P(None, 'dp')
- position_copy: bfloat16 [196, 768], P(None, 'dp')
The draws below stay inside these ranges and needn't reach their ends.
Inputs may be any that keep to these rules, and one draw needn't show every extreme that they name: `mask_rank`: each image's row is a permutation of the patch indices. `image_count`: some index of dp holds 8 live images in every draw. `vectors`: rows 0 and 2 (gains) lie in 0.4 to 1.6; rows 1, 3, 4 and 5 in -1.8 to 1.8; row 6 (the mask token) in -6 to 6.
All inputs are finite; a program needn't handle non-finite values.
Results may differ from the reference program's by a relative error of at most 0.015.
Values may be sent and summed in bfloat16 or wider, within the bound.
No kernel may reach another device: no remote copies, remote signals or barrier semaphores. Data moves between devices by JAX's collectives and lax.ppermute only.
A program may use at most 128 MiB of HBM per device.

```python
import math
import jax
import jax.numpy as jnp
from jax import lax

D = 768
HEADS = 12
HEAD_DIM = 64
FF = 3072
PATCHES = 196
IMG_CAP = 8
STEP = 7
IMAGES = 64
TOKENS = 12544
N_DP = 8
N_TENSOR = 4


def draw_vectors(key, part):
    base = jnp.clip(jax.random.normal(key, (7, D), jnp.float32), -6.0, 6.0)
    rows = lax.broadcasted_iota(jnp.int32, (7, D), 0)
    gains = 1.0 + 0.3 * jnp.clip(base, -2.0, 2.0)
    shifts = 0.3 * base
    picked = jnp.where(rows == 6, base, shifts)
    return jnp.where((rows == 0) | (rows == 2), gains, picked).astype(jnp.float32)


def draw_image_count(key, part):
    counts = jax.random.randint(key, (N_DP,), 1, IMG_CAP + 1)
    chosen = jax.random.randint(jax.random.fold_in(key, 7), (), 0, N_DP)
    places = jnp.arange(N_DP, dtype=jnp.int32)
    return jnp.where(places == chosen, IMG_CAP, counts).astype(jnp.int32)


def place_ends(result, own_key, low, largest):
    dims = result.shape
    spot = [jax.random.randint(jax.random.fold_in(own_key, axis), (), 0, dims[axis]) for axis in range(len(dims))]
    result = result.at[tuple(spot)].set(low)
    longest = dims.index(max(dims))
    spot[longest] = (spot[longest] + 1) % dims[longest]
    return result.at[tuple(spot)].set(largest)


def block_levels(own_key, shape, cuts, least, largest):
    loudness = 1.0
    for dim, parts in cuts:
        draws = jax.random.uniform(jax.random.fold_in(jax.random.fold_in(own_key, 6), dim), (parts,), jnp.float32, least / len(cuts), largest / len(cuts))
        loudness = loudness * jnp.repeat(jnp.exp(draws), shape[dim] // parts).reshape((-1,) + (1,) * (len(shape) - 1 - dim))
    return loudness


def gaussian(key, shape, spread, most, shards=(), kind=jnp.bfloat16):
    array = jax.random.normal(key, shape, jnp.float32) * spread
    if len(shards) > 0:
        array = block_levels(key, shape, shards, -0.22, 0.18) * array
    return jnp.clip(array, min=-most, max=most).astype(kind)


def setup_inputs(seed: int = 0) -> dict:
    streams_of = jax.random.split(jax.random.key(seed), 30)
    patches = gaussian(streams_of[0], (IMAGES, PATCHES, D), 1.0, 6.0, ((0, 8),))
    cotangent = gaussian(streams_of[1], (IMAGES, PATCHES, D), 1.0, 6.0, ((0, 8),))
    mask_rank = jax.vmap(lambda own: jax.random.permutation(own, PATCHES))(jax.random.split(streams_of[2], IMAGES)).reshape((IMAGES, PATCHES)).astype(jnp.int32)
    mask_count = place_ends(jax.random.randint(streams_of[3], (IMAGES,), 2 * PATCHES // 5, 4 * PATCHES // 5 + 1), jax.random.fold_in(streams_of[3], 1), 2 * PATCHES // 5, (4 * PATCHES // 5 + 1) - 1).astype(jnp.int32)
    image_count = draw_image_count(jax.random.fold_in(streams_of[29], 71), 0)
    entry_weight = gaussian(streams_of[5], (3, D, D), D ** -0.5, 0.21875, ((1, 8), (2, 4)), jnp.float32)
    entry_moment = gaussian(streams_of[6], (3, D, D), (0.03 * TOKENS ** 0.5), 20.0, ((1, 8), (2, 4)), jnp.float32)
    entry_second = jnp.clip(jnp.exp(math.log(6.77376) - 2.7652086 * jax.random.uniform(streams_of[7], (3, D, D), jnp.float32) ** block_levels(streams_of[7], (3, D, D), ((1, 8), (2, 4)), -0.2, 0.2)), 0.426496, 6.77376)
    entry_bias = gaussian(streams_of[8], (2, N_TENSOR, D // N_TENSOR), 0.3, 4.0, ((1, 4), (2, 8)), jnp.float32)
    entry_bias_moment = gaussian(streams_of[9], (2, N_TENSOR, D // N_TENSOR), (0.03 * TOKENS ** 0.5), 20.0, ((1, 4), (2, 8)), jnp.float32)
    entry_bias_second = jnp.clip(jnp.exp(math.log(6.77376) - 2.7652086 * jax.random.uniform(streams_of[10], (2, N_TENSOR, D // N_TENSOR), jnp.float32) ** block_levels(streams_of[10], (2, N_TENSOR, D // N_TENSOR), ((1, 4), (2, 8)), -0.2, 0.2)), 0.426496, 6.77376)
    exit_weight = gaussian(streams_of[11], (D, D), (D // 8) ** -0.5, 0.625, ((0, 4), (1, 8)), jnp.float32)
    exit_moment = gaussian(streams_of[12], (D, D), (0.03 * TOKENS ** 0.5), 20.0, ((0, 4), (1, 8)), jnp.float32)
    exit_second = jnp.clip(jnp.exp(math.log(6.77376) - 2.7652086 * jax.random.uniform(streams_of[13], (D, D), jnp.float32) ** block_levels(streams_of[13], (D, D), ((0, 4), (1, 8)), -0.2, 0.2)), 0.426496, 6.77376)
    expand_weight = gaussian(streams_of[14], (D, FF), D ** -0.5, 0.21875, ((0, 8), (1, 4)), jnp.float32)
    expand_moment = gaussian(streams_of[15], (D, FF), (0.03 * TOKENS ** 0.5), 20.0, ((0, 8), (1, 4)), jnp.float32)
    expand_second = jnp.clip(jnp.exp(math.log(6.77376) - 2.7652086 * jax.random.uniform(streams_of[16], (D, FF), jnp.float32) ** block_levels(streams_of[16], (D, FF), ((0, 8), (1, 4)), -0.2, 0.2)), 0.426496, 6.77376)
    expand_bias = gaussian(streams_of[17], (N_TENSOR, FF // N_TENSOR), 0.3, 4.0, ((0, 4), (1, 8)), jnp.float32)
    expand_bias_moment = gaussian(streams_of[18], (N_TENSOR, FF // N_TENSOR), (0.03 * TOKENS ** 0.5), 20.0, ((0, 4), (1, 8)), jnp.float32)
    expand_bias_second = jnp.clip(jnp.exp(math.log(6.77376) - 2.7652086 * jax.random.uniform(streams_of[19], (N_TENSOR, FF // N_TENSOR), jnp.float32) ** block_levels(streams_of[19], (N_TENSOR, FF // N_TENSOR), ((0, 4), (1, 8)), -0.2, 0.2)), 0.426496, 6.77376)
    reduce_weight = gaussian(streams_of[20], (FF, D), FF ** -0.5, 0.109375, ((0, 4), (1, 8)), jnp.float32)
    reduce_moment = gaussian(streams_of[21], (FF, D), (0.03 * TOKENS ** 0.5), 20.0, ((0, 4), (1, 8)), jnp.float32)
    reduce_second = jnp.clip(jnp.exp(math.log(6.77376) - 2.7652086 * jax.random.uniform(streams_of[22], (FF, D), jnp.float32) ** block_levels(streams_of[22], (FF, D), ((0, 4), (1, 8)), -0.2, 0.2)), 0.426496, 6.77376)
    vectors = draw_vectors(jax.random.fold_in(streams_of[29], 71), 0)
    vectors_moment = gaussian(streams_of[24], (7, D), (0.1 * TOKENS ** 0.5), 64.0, ((1, 8),), jnp.float32)
    vectors_second = jnp.clip(jnp.exp(math.log(75.264) - 2.7725887 * jax.random.uniform(streams_of[25], (7, D), jnp.float32) ** block_levels(streams_of[25], (7, D), ((1, 8),), -0.2, 0.2)), 4.704, 75.264)
    position = gaussian(streams_of[26], (PATCHES, D), 0.3, 4.0, ((1, 8),), jnp.float32)
    position_moment = gaussian(streams_of[27], (PATCHES, D), (0.15 * IMAGES ** 0.5), 4.0, ((1, 8),), jnp.float32)
    position_second = jnp.clip(jnp.exp(math.log(0.512) - 2.0794415 * jax.random.uniform(streams_of[28], (PATCHES, D), jnp.float32) ** block_levels(streams_of[28], (PATCHES, D), ((1, 8),), -0.2, 0.2)), 0.064, 0.512)
    return {"patches": patches, "cotangent": cotangent, "mask_rank": mask_rank, "mask_count": mask_count, "image_count": image_count, "entry_weight": entry_weight, "entry_moment": entry_moment, "entry_second": entry_second, "entry_bias": entry_bias, "entry_bias_moment": entry_bias_moment, "entry_bias_second": entry_bias_second, "exit_weight": exit_weight, "exit_moment": exit_moment, "exit_second": exit_second, "expand_weight": expand_weight, "expand_moment": expand_moment, "expand_second": expand_second, "expand_bias": expand_bias, "expand_bias_moment": expand_bias_moment, "expand_bias_second": expand_bias_second, "reduce_weight": reduce_weight, "reduce_moment": reduce_moment, "reduce_second": reduce_second, "vectors": vectors, "vectors_moment": vectors_moment, "vectors_second": vectors_second, "position": position, "position_moment": position_moment, "position_second": position_second}


@jax.custom_vjp
def low(v):
    return lax.optimization_barrier(v.astype(jnp.bfloat16)).astype(jnp.float32)

@jax.custom_vjp
def low_back(v):
    return v

def low_keep(v):
    return (low(v), None)

def low_pass(kept, grad):
    return (grad,)

def back_keep(v):
    return (v, None)

def back_low(kept, grad):
    return (low(grad),)
low.defvjp(low_keep, low_pass)
low_back.defvjp(back_keep, back_low)
NORM_EPS = 1e-06
HIGHEST = lax.Precision.HIGHEST

def layer_norm(rows, gain, shift):
    centered = rows - lax.optimization_barrier(jnp.mean(rows, -1, keepdims=True))
    inverse = lax.rsqrt(lax.optimization_barrier(jnp.mean(centered * centered, -1, keepdims=True)) + NORM_EPS)
    return centered * inverse * gain + shift

def attend(triple):
    query, keys, values = (triple[0], triple[1], triple[2])
    scores = low_back(jnp.einsum('qhd,khd->hqk', query, keys, precision=HIGHEST) * HEAD_DIM ** (-0.5))
    probs = jax.nn.softmax(scores, -1)
    return jnp.einsum('hqk,khd->qhd', low(probs), values, precision=HIGHEST)

def adamw(master, moment, second, grad, rate, decay):
    moment = 0.9 * moment + 0.1 * grad
    second = 0.999 * second + 0.001 * grad * grad
    fixed_first = moment / (1.0 - 0.9 ** STEP)
    fixed_second = second / (1.0 - 0.999 ** STEP)
    master = master - rate * (fixed_first / (jnp.sqrt(fixed_second) + 1e-08) + decay * master)
    return (master, moment, second, master.astype(jnp.bfloat16))

def reference(patches, cotangent, mask_rank, mask_count, image_count, entry_weight, entry_moment, entry_second, entry_bias, entry_bias_moment, entry_bias_second, exit_weight, exit_moment, exit_second, expand_weight, expand_moment, expand_second, expand_bias, expand_bias_moment, expand_bias_second, reduce_weight, reduce_moment, reduce_second, vectors, vectors_moment, vectors_second, position, position_moment, position_second):
    images = patches.shape[0]
    slots = jnp.arange(images, dtype=jnp.int32)
    live = (slots % IMG_CAP < image_count[slots // IMG_CAP]).astype(jnp.float32)
    masked = mask_rank < mask_count[:, None]

    def forward(w_entry, b_entry, w_exit, w_expand, b_expand, w_reduce, table, place, inputs):
        start = (jnp.where(masked[..., None], table[6], inputs) + place[None]).reshape(images * PATCHES, D)
        normed = low(layer_norm(start, table[0], table[1]))
        flat_bias = b_entry.reshape(2, D)
        shifts = jnp.stack([flat_bias[0], jnp.zeros((D,), jnp.float32), flat_bias[1]])
        qkv = jnp.einsum('td,jde->jte', normed, w_entry, precision=HIGHEST) + shifts[:, None, :]
        qkv = low(low_back(qkv))
        heads = qkv.reshape(3, images, PATCHES, HEADS, HEAD_DIM).transpose(1, 0, 2, 3, 4)
        mixed = lax.map(jax.checkpoint(attend), heads)
        mixed = low(low_back(mixed.reshape(images * PATCHES, D)))
        branch = low_back(jnp.dot(mixed, w_exit, precision=HIGHEST))
        middle = start + branch + table[4]
        normed_two = low(layer_norm(middle, table[2], table[3]))
        upper = low_back(jnp.dot(normed_two, w_expand, precision=HIGHEST) + b_expand.reshape(FF))
        active = low(jax.nn.gelu(upper, approximate=False))
        branch_two = low_back(jnp.dot(active, w_reduce, precision=HIGHEST))
        return (middle + branch_two + table[5]).reshape(images, PATCHES, D)
    masters = (entry_weight, entry_bias, exit_weight, expand_weight, expand_bias, reduce_weight, vectors, position)
    rounded = tuple((low(master) for master in masters))
    output, pullback = jax.vjp(forward, *rounded, patches.astype(jnp.float32))
    grads = pullback(cotangent.astype(jnp.float32) * live[:, None, None])
    block_out = jnp.where(live[:, None, None] > 0.5, output, 0.0).astype(jnp.bfloat16)
    patch_grad = grads[8].astype(jnp.bfloat16)
    entry = adamw(entry_weight, entry_moment, entry_second, grads[0], 0.05, 0.05)
    entry_b = adamw(entry_bias, entry_bias_moment, entry_bias_second, grads[1], 0.3, 0.0)
    exits = adamw(exit_weight, exit_moment, exit_second, grads[2], 0.05, 0.05)
    expand = adamw(expand_weight, expand_moment, expand_second, grads[3], 0.05, 0.05)
    expand_b = adamw(expand_bias, expand_bias_moment, expand_bias_second, grads[4], 0.3, 0.0)
    reduce_w = adamw(reduce_weight, reduce_moment, reduce_second, grads[5], 0.05, 0.05)
    table_new = adamw(vectors, vectors_moment, vectors_second, grads[6], 0.3, 0.0)
    place_new = adamw(position, position_moment, position_second, grads[7], 0.1, 0.0)
    return (block_out, patch_grad, entry[0], entry[1], entry[2], entry[3], entry_b[0], entry_b[1], entry_b[2], entry_b[3], exits[0], exits[1], exits[2], exits[3], expand[0], expand[1], expand[2], expand[3], expand_b[0], expand_b[1], expand_b[2], expand_b[3], reduce_w[0], reduce_w[1], reduce_w[2], reduce_w[3], table_new[0], table_new[1], table_new[2], table_new[3], place_new[0], place_new[1], place_new[2], place_new[3])
```

```python
import functools

import jax
import jax.numpy as jnp
from jax import lax
from jax.experimental import pallas as pl
from jax.experimental.pallas import tpu as pltpu
from jax.sharding import PartitionSpec as P

HEAD_DIM = 64
STEP = 7
NORM_EPS = 1e-06
HALF = jnp.bfloat16
SINGLE = jnp.float32
VMEM = pl.BlockSpec(memory_space=pltpu.VMEM)
SMEM = pl.BlockSpec(memory_space=pltpu.SMEM)
ANY = pl.BlockSpec(memory_space=pl.ANY)
CHUNK = 16
SMALL_ROWS = 80
PLACE_ROWS = 64


def adamw(master, moment, second, grad, rate, decay):
    moment = 0.9 * moment + 0.1 * grad
    second = 0.999 * second + 0.001 * grad * grad
    fixed_first = moment / (1.0 - 0.9**STEP)
    fixed_second = second / (1.0 - 0.999**STEP)
    master = master - rate * (fixed_first / (jnp.sqrt(fixed_second) + 1e-08) + decay * master)
    return (master, moment, second, master.astype(jnp.bfloat16))


def dot(left, right):
    return jnp.dot(left, right, preferred_element_type=SINGLE)


def row_dot(left, right):
    return lax.dot_general(left, right, (((1,), (1,)), ((), ())), preferred_element_type=SINGLE)


def column_dot(left, right):
    return lax.dot_general(left, right, (((0,), (0,)), ((), ())), preferred_element_type=SINGLE)


def kernel_call(body, outs, operands, scratch, flops, name):
    size = lambda a: a.size * a.dtype.itemsize
    moved = sum(size(a) for a, _ in operands) + sum(size(a) for a, _ in outs)
    return pl.pallas_call(
        body,
        out_shape=[a for a, _ in outs],
        in_specs=[spec for _, spec in operands],
        out_specs=[spec for _, spec in outs],
        scratch_shapes=scratch,
        cost_estimate=pl.CostEstimate(flops=flops, bytes_accessed=moved, transcendentals=0),
        name=name,
    )(*[a for a, _ in operands])


def shape(dims, kind):
    return jax.ShapeDtypeStruct(dims, kind)


class Direct:
    def __init__(self, n_dp, n_tensor):
        self.n_dp = n_dp
        self.n_tensor = n_tensor

    def flip(self, array, axis, bits):
        count = self.n_dp if axis == "dp" else self.n_tensor
        return lax.ppermute(array, axis, [(i, i ^ bits) for i in range(count)])

    def along(self, array, name):
        axis, bits = {
            "core": ("tensor", 1),
            "x": ("tensor", 2),
            "y": ("dp", 1),
            "z1": ("dp", 2),
            "z2": ("dp", 4),
            "z3": ("dp", 6),
        }[name]
        return self.flip(array, axis, bits)

    def gather(self, shard):
        blocks = [shard] + [self.along(shard, f"z{k}") for k in (1, 2, 3)]
        first = jnp.stack(blocks[:2])
        last = jnp.stack(blocks[2:])
        first_y = self.along(first, "y")
        last_x = self.along(last, "x")
        chip = [
            (first, 0, 0, (0, 1)),
            (first_y, 0, 1, (0, 1)),
            (self.along(first, "x"), 1, 0, (0, 1)),
            (self.along(first_y, "x"), 1, 1, (0, 1)),
            (last, 0, 0, (2, 3)),
            (last_x, 1, 0, (2, 3)),
            (self.along(last, "y"), 0, 1, (2, 3)),
            (self.along(last_x, "y"), 1, 1, (2, 3)),
        ]
        pieces = []
        for core in (0, 1):
            for piece, x, y, steps in chip:
                held = self.along(piece, "core") if core else piece
                pieces.append((held, [(2 * x + core, 2 * k + y) for k in steps]))
        return pieces

    def grad_layout(self):
        layout = []
        for core in (0, 1):
            for half, steps in enumerate(((0, 1), (2, 3))):
                for first in (0, 1):
                    blocks = []
                    for second in (0, 1):
                        x, y = (first, second) if half == 0 else (second, first)
                        for k in steps:
                            blocks.append((2 * x + core, 2 * k + y))
                    layout.append(blocks)
        return layout

    def reduce(self, outs):
        sent = [self.along(piece, "core") for piece in outs[4:]]
        held = [add(kept, came) for kept, came in zip(outs[:4], sent)]
        done = []
        for half, (one, two) in enumerate((("x", "y"), ("y", "x"))):
            keep, send = held[2 * half], held[2 * half + 1]
            came = self.along(send, one)
            near = add(keep[:2], came[:2])
            far = add(keep[2:], came[2:])
            done.append(add(near, self.along(far, two)))
        near, far = done
        return [
            near[0],
            self.along(near[1], "z1"),
            self.along(far[0], "z2"),
            self.along(far[1], "z3"),
        ]


def add(left, right):
    return (left.astype(SINGLE) + right.astype(SINGLE)).astype(HALF)


def load_pieces(place_ref, piece_refs, spots, dst_ref, sems):
    copies = []
    for ref, where in zip(piece_refs, spots):
        for j, (t_flip, dp_flip) in enumerate(where):
            t = place_ref[1] ^ t_flip
            if dp_flip is None:
                dst = dst_ref.at[t]
            else:
                rows = ref.shape[1]
                row = pl.multiple_of((place_ref[0] ^ dp_flip) * rows, rows)
                dst = dst_ref.at[t, pl.ds(row, rows), :]
            copies.append(pltpu.make_async_copy(ref.at[j], dst, sems.at[len(copies)]))
    for copy in copies:
        copy.start()
    return copies


def store_grads(place_ref, src_ref, out_refs, layout, rows, sems):
    copies = []
    for ref, where in zip(out_refs, layout):
        for j, (t_flip, dp_flip) in enumerate(where):
            t = place_ref[1] ^ t_flip
            if dp_flip is None:
                src = src_ref.at[t]
            else:
                row = pl.multiple_of((place_ref[0] ^ dp_flip) * rows, rows)
                src = src_ref.at[t, pl.ds(row, rows), :]
            copies.append(pltpu.make_async_copy(src, ref.at[j], sems.at[len(copies)]))
    for copy in copies:
        copy.start()
    return copies


def wait_all(copies):
    for copy in copies:
        copy.wait()


def fold(rows):
    return rows[:8] + rows[8:]


def norm_scaled(rows):
    width = rows.shape[-1]
    centered = rows - jnp.sum(rows, -1, keepdims=True) * (1.0 / width)
    inverse = lax.rsqrt(jnp.sum(centered * centered, -1, keepdims=True) * (1.0 / width) + NORM_EPS)
    return centered * inverse, inverse


def norm_grad(grad, scaled, inverse, gain):
    width = grad.shape[-1]
    scale = 1.0 / width
    e = grad * gain
    mean_e = jnp.sum(e, -1, keepdims=True) * scale
    mean_cross = jnp.sum(e * scaled, -1, keepdims=True) * scale
    return inverse * (e - mean_e - scaled * mean_cross)


def start_body(
    images, patches, pad, packed, place_ref, patch_ref, cot_ref, mask_ref, live_ref, *rest
):
    if packed:
        (small_ref, start_ref, normed_ref, low_ref, table_ref, entry_ref, expand_ref, pair, both, spot, sems) = rest
    else:
        (spot, table_in, entry_in, expand_in, start_ref, normed_ref, low_ref, table_ref, entry_ref, expand_ref, pair, both, sems) = rest
    t = place_ref[1]
    copies = [
        pltpu.make_async_copy(patch_ref.at[pl.ds(images * t, images)], pair, sems.at[0]),
        pltpu.make_async_copy(cot_ref.at[pl.ds(images * t, images)], both, sems.at[1]),
    ]
    for copy in copies:
        copy.start()
    n_tensor = entry_ref.shape[0]
    columns = entry_ref.shape[2] // 3
    entry_ref[...] = jnp.zeros_like(entry_ref)
    if packed:
        n_dp = small_ref.shape[0] // n_tensor
        part = spot.shape[1] // n_dp
        for dp_at in range(n_dp):
            for t_at in range(n_tensor):
                t_flip = t ^ t_at
                dp_flip = place_ref[0] ^ dp_at
                slot = (t_flip & 1) * 16 + (t_flip >> 1) * 8 + (dp_flip & 1) * 4 + (dp_flip >> 1)
                block = small_ref[slot].astype(SINGLE)
                spot[PLACE_ROWS * t_at : PLACE_ROWS * (t_at + 1), part * dp_at : part * (dp_at + 1)] = block[:PLACE_ROWS, :part]
                bias = block[PLACE_ROWS : PLACE_ROWS + 8]
                expand_ref[t_at, :, part * dp_at : part * (dp_at + 1)] = bias[0:1, :part]
                own = part // n_tensor
                entry_ref[t_at, :, own * dp_at : own * (dp_at + 1)] = bias[1:2, :own]
                entry_ref[t_at, :, 2 * columns + own * dp_at : 2 * columns + own * (dp_at + 1)] = bias[2:3, :own]
        table_ref[...] = spot[200:208, :]
    else:
        table_ref[...] = table_in[...]
        entry_ref[...] = entry_in[...]
        expand_ref[...] = expand_in[...]
    wait_all(copies)
    start_ref[...] = jnp.zeros_like(start_ref)
    token = table_ref[6:7, :]
    low_ref[...] = jnp.zeros_like(low_ref)
    for i in range(images):
        rows = pl.ds(i * pad, patches)
        picked = jnp.where(mask_ref[rows, :] > 0.5, token, pair[i].astype(SINGLE))
        start_ref[rows, :] = picked + spot[:patches, :]
        low_ref[rows, :] = (both[i].astype(SINGLE) * live_ref[i]).astype(HALF)
    gain, shift = table_ref[0:1, :], table_ref[1:2, :]

    def one(j, carry):
        rows = pl.ds(pl.multiple_of(j * CHUNK, CHUNK), CHUNK)
        scaled, _ = norm_scaled(start_ref[rows, :])
        normed_ref[rows, :] = (scaled * gain + shift).astype(HALF)
        return carry

    lax.fori_loop(0, start_ref.shape[0] // CHUNK, one, 0)


def attend_body(
    images, patches, pad, spots, place_ref, normed_ref, bias_ref, *rest
):
    n = len(spots)
    piece_refs = rest[:n]
    qkv_ref, probs_ref, mixed_ref, full_ref, held, sems, out_sem = rest[n:]
    columns = mixed_ref.shape[2]
    heads = columns // HEAD_DIM
    wait_all(load_pieces(place_ref, piece_refs, spots, held, sems))
    out = pltpu.make_async_copy(held, full_ref, out_sem)
    out.start()
    lanes = lax.broadcasted_iota(jnp.int32, (pad, pad), 1)

    def one(t, carry):
        qkv = dot(normed_ref[...], held[t, :, : 3 * columns]) + bias_ref[t]
        qkv_ref[t] = qkv.astype(HALF)
        for i in range(images):
            rows = slice(i * pad, (i + 1) * pad)
            for h in range(heads):
                at = h * HEAD_DIM
                query = qkv_ref[t, rows, at : at + HEAD_DIM]
                keys = qkv_ref[t, rows, columns + at : columns + at + HEAD_DIM]
                values = qkv_ref[t, rows, 2 * columns + at : 2 * columns + at + HEAD_DIM]
                scores = row_dot(query, keys) * HEAD_DIM ** (-0.5)
                scores = jnp.where(lanes < patches, scores, -1e30)
                risen = jnp.exp(scores - jnp.max(scores, -1, keepdims=True))
                probs = (risen * (1.0 / jnp.sum(risen, -1, keepdims=True))).astype(HALF)
                probs_ref[t, i * heads + h] = probs
                mixed_ref[t, rows, at : at + HEAD_DIM] = dot(probs, values).astype(HALF)
        return carry

    lax.fori_loop(0, held.shape[0], one, 0)
    out.wait()


def up_body(spots, layout, rows_out, place_ref, start_ref, mixed_ref, full_ref, low_ref, table_ref, bias_ref, *rest):
    n, m = len(spots), len(layout)
    piece_refs = rest[:n]
    middle_ref, normed_ref, active_ref, slope_ref, expand_ref = rest[n : n + 5]
    out_refs = rest[n + 5 : n + 5 + m]
    held, upper, grads, sems, out_sem, grad_sems = rest[n + 5 + m :]
    n_tensor = held.shape[0]
    tokens = start_ref.shape[0]
    columns = mixed_ref.shape[2]
    copies = load_pieces(place_ref, piece_refs, spots, held, sems)
    middle_ref[...] = start_ref[...] + table_ref[4:5, :]

    def leave(t, carry):
        middle_ref[...] += row_dot(mixed_ref[t], full_ref[t, :, 3 * columns :])
        return carry

    lax.fori_loop(0, n_tensor, leave, 0)
    gain, shift = table_ref[2:3, :], table_ref[3:4, :]

    def one(j, carry):
        rows = pl.ds(pl.multiple_of(j * CHUNK, CHUNK), CHUNK)
        scaled, _ = norm_scaled(middle_ref[rows, :])
        normed_ref[rows, :] = (scaled * gain + shift).astype(HALF)
        return carry

    lax.fori_loop(0, tokens // CHUNK, one, 0)
    wait_all(copies)
    out = pltpu.make_async_copy(held, expand_ref, out_sem)
    out.start()

    def up(t, carry):
        upper[...] = dot(normed_ref[...], held[t]) + bias_ref[t]

        def bend(j, inner):
            rows = pl.ds(pl.multiple_of(j * CHUNK, CHUNK), CHUNK)
            u = upper[rows, :]
            cdf = 0.5 * (1.0 + lax.erf(u * 0.7071067811865476))
            active_ref[t, rows, :] = (u * cdf).astype(HALF)
            slope = cdf + u * (jnp.exp(u * u * -0.5) * 0.3989422804014327)
            slope_ref[t, rows, :] = slope.astype(HALF)
            return inner

        lax.fori_loop(0, tokens // CHUNK, bend, 0)
        grads[t] = column_dot(low_ref[...], active_ref[t]).astype(HALF)
        return carry

    lax.fori_loop(0, n_tensor, up, 0)
    wait_all(store_grads(place_ref, grads, out_refs, layout, rows_out, grad_sems))
    out.wait()


def down_body(spots, layout, rows_out, place_ref, low_ref, slope_ref, normed_ref, *rest):
    n, m = len(spots), len(layout)
    piece_refs = rest[:n]
    grad_upper_ref, reduce_ref, sums_ref = rest[n : n + 3]
    out_refs = rest[n + 3 : n + 3 + m]
    held, upper, grads, sems, out_sem, grad_sems = rest[n + 3 + m :]
    n_tensor = held.shape[0]
    tokens, width = low_ref.shape
    wait_all(load_pieces(place_ref, piece_refs, spots, held, sems))
    out = pltpu.make_async_copy(held, reduce_ref, out_sem)
    out.start()

    def up(t, carry):
        upper[...] = dot(low_ref[...], held[t])

        def bend(j, total):
            rows = pl.ds(pl.multiple_of(j * CHUNK, CHUNK), CHUNK)
            grad = (upper[rows, :] * slope_ref[t, rows, :].astype(SINGLE)).astype(HALF)
            grad_upper_ref[t, rows, :] = grad
            return total + fold(grad.astype(SINGLE))

        total = lax.fori_loop(0, tokens // CHUNK, bend, jnp.zeros((8, upper.shape[1]), SINGLE))
        sums_ref[t] = total
        grads[t] = column_dot(normed_ref[...], grad_upper_ref[t]).astype(HALF)
        return carry

    lax.fori_loop(0, n_tensor, up, 0)
    wait_all(store_grads(place_ref, grads, out_refs, layout, rows_out, grad_sems))
    out.wait()


def middle_body(grad_upper_ref, expand_ref, full_ref, middle_ref, low_ref, table_ref, grad_ref, half_ref, mixed_ref, sums_ref, normed_grad):
    n_tensor, tokens, columns = mixed_ref.shape
    normed_grad[...] = row_dot(grad_upper_ref[0], expand_ref[0])

    def back(t, carry):
        normed_grad[...] += row_dot(grad_upper_ref[t], expand_ref[t])
        return carry

    lax.fori_loop(1, n_tensor, back, 0)
    gain = table_ref[2:3, :]

    def one(j, carry):
        rows = pl.ds(pl.multiple_of(j * CHUNK, CHUNK), CHUNK)
        scaled, inverse = norm_scaled(middle_ref[rows, :])
        grad = normed_grad[rows, :]
        low = low_ref[rows, :].astype(SINGLE)
        out = low + norm_grad(grad, scaled, inverse, gain)
        grad_ref[rows, :] = out
        half_ref[rows, :] = out.astype(HALF)
        parts = (grad * scaled, grad, out, low)
        return tuple(c + fold(p) for c, p in zip(carry, parts))

    zero = jnp.zeros((8, low_ref.shape[1]), SINGLE)
    totals = lax.fori_loop(0, tokens // CHUNK, one, (zero,) * 4)
    for row, total in enumerate(totals):
        sums_ref[row] = total

    def mix(t, carry):
        mixed_ref[t] = dot(half_ref[...], full_ref[t, :, 3 * columns :]).astype(HALF)
        return carry

    lax.fori_loop(0, n_tensor, mix, 0)


def attend_back_body(images, pad, layout, rows_out, place_ref, qkv_ref, probs_ref, grad_mixed_ref, normed_ref, half_ref, mixed_ref, *rest):
    m = len(layout)
    grad_ref, sums_ref = rest[:2]
    out_refs = rest[2 : 2 + m]
    grads, grad_sems = rest[2 + m :]
    n_tensor, tokens, columns = mixed_ref.shape
    heads = columns // HEAD_DIM
    scale = HEAD_DIM ** (-0.5)

    def one(t, carry):
        for i in range(images):
            rows = slice(i * pad, (i + 1) * pad)
            for h in range(heads):
                at = h * HEAD_DIM
                query = qkv_ref[t, rows, at : at + HEAD_DIM]
                keys = qkv_ref[t, rows, columns + at : columns + at + HEAD_DIM]
                values = qkv_ref[t, rows, 2 * columns + at : 2 * columns + at + HEAD_DIM]
                grad = grad_mixed_ref[t, rows, at : at + HEAD_DIM]
                low = probs_ref[t, i * heads + h]
                probs = low.astype(SINGLE)
                grad_ref[t, rows, 2 * columns + at : 2 * columns + at + HEAD_DIM] = column_dot(low, grad).astype(HALF)
                grad_probs = row_dot(grad, values)
                inner = jnp.sum(probs * grad_probs, -1, keepdims=True)
                grad_scores = (probs * (grad_probs - inner)).astype(HALF)
                grad_ref[t, rows, at : at + HEAD_DIM] = (dot(grad_scores, keys) * scale).astype(HALF)
                grad_ref[t, rows, columns + at : columns + at + HEAD_DIM] = (column_dot(grad_scores, query) * scale).astype(HALF)
        total = grad_ref[t].astype(SINGLE)
        sums_ref[t] = jnp.sum(total.reshape(tokens // 8, 8, 3 * columns), 0)
        grads[t, :, : 3 * columns] = column_dot(normed_ref[...], grad_ref[t]).astype(HALF)
        grads[t, :, 3 * columns :] = column_dot(half_ref[...], mixed_ref[t]).astype(HALF)
        return carry

    lax.fori_loop(0, n_tensor, one, 0)
    wait_all(store_grads(place_ref, grads, out_refs, layout, rows_out, grad_sems))


def output_body(images, patches, pad, live_ref, middle_ref, active_ref, reduce_ref, table_ref, out_ref, total, low):
    n_tensor = active_ref.shape[0]
    total[...] = middle_ref[...] + table_ref[5:6, :]

    def one(t, carry):
        total[...] += row_dot(active_ref[t], reduce_ref[t])
        return carry

    lax.fori_loop(0, n_tensor, one, 0)
    for i in range(images):
        out_ref[i] = (total[pl.ds(i * pad, patches), :] * live_ref[i]).astype(HALF)


def end_body(images, patches, pad, packed, place_ref, grad_qkv_ref, full_ref, start_ref, grad_middle_ref, mask_ref, table_ref, sums_two_ref, sums_entry_ref, sums_expand_ref, *rest):
    if packed:
        out_ref, small_ref, normed_grad, ended, low, spot = rest
    else:
        out_ref, spot, entry_ref, expand_ref, normed_grad, ended, low = rest
    n_tensor = grad_qkv_ref.shape[0]
    tokens, width = start_ref.shape
    columns = grad_qkv_ref.shape[2] // 3
    normed_grad[...] = row_dot(grad_qkv_ref[0], full_ref[0, :, : 3 * columns])

    def back(t, carry):
        normed_grad[...] += row_dot(grad_qkv_ref[t], full_ref[t, :, : 3 * columns])
        return carry

    lax.fori_loop(1, n_tensor, back, 0)
    gain = table_ref[0:1, :]

    def one(j, carry):
        rows = pl.ds(pl.multiple_of(j * CHUNK, CHUNK), CHUNK)
        scaled, inverse = norm_scaled(start_ref[rows, :])
        grad = normed_grad[rows, :]
        out = grad_middle_ref[rows, :] + norm_grad(grad, scaled, inverse, gain)
        ended[rows, :] = out
        masked = mask_ref[rows, :] > 0.5
        low[rows, :] = jnp.where(masked, 0.0, out).astype(HALF)
        parts = (grad * scaled, grad, jnp.where(masked, out, 0.0))
        return tuple(c + fold(p) for c, p in zip(carry, parts))

    zero = jnp.zeros((8, width), SINGLE)
    totals = lax.fori_loop(0, tokens // CHUNK, one, (zero,) * 3)
    for i in range(images):
        out_ref[i] = low[pl.ds(i * pad, patches), :]
    place = ended[:pad, :]
    for i in range(1, images):
        place = place + ended[i * pad : (i + 1) * pad, :]
    column = lambda total: jnp.sum(total, 0, keepdims=True)
    spot[...] = jnp.zeros_like(spot)
    spot[:pad, :] = place
    rows = [column(totals[0]), column(totals[1])]
    rows += [column(sums_two_ref[row]) for row in range(4)]
    rows += [column(totals[2])]
    for row, total in enumerate(rows):
        spot[200 + row : 201 + row, :] = total
    if not packed:
        for t in range(n_tensor):
            entry_ref[t] = column(sums_entry_ref[t])
            expand_ref[t] = column(sums_expand_ref[t])
        return
    n_dp = small_ref.shape[0] // n_tensor
    part = width // n_dp
    own = part // n_tensor
    small_ref[...] = jnp.zeros_like(small_ref)
    for t_at in range(n_tensor):
        entry = column(sums_entry_ref[t_at])
        expand = column(sums_expand_ref[t_at])
        for dp_at in range(n_dp):
            t_flip = place_ref[1] ^ t_at
            dp_flip = place_ref[0] ^ dp_at
            slot = (t_flip & 1) * 16 + (t_flip >> 1) * 8 + (dp_flip & 1) * 4 + (dp_flip >> 1)
            block = spot[PLACE_ROWS * t_at : PLACE_ROWS * (t_at + 1), part * dp_at : part * (dp_at + 1)]
            small_ref[slot, :PLACE_ROWS, :part] = block
            small_ref[slot, PLACE_ROWS : PLACE_ROWS + 1, :part] = expand[:, part * dp_at : part * (dp_at + 1)]
            small_ref[slot, PLACE_ROWS + 1 : PLACE_ROWS + 2, :own] = entry[:, own * dp_at : own * (dp_at + 1)]
            small_ref[slot, PLACE_ROWS + 2 : PLACE_ROWS + 3, :own] = entry[:, 2 * columns + own * dp_at : 2 * columns + own * (dp_at + 1)]


def place_body(images, place_ref, own_ref, core_ref, x_ref, far_ref, out_ref):
    t = place_ref[1]
    for flip, ref in enumerate((own_ref, core_ref, x_ref, far_ref)):
        out_ref[pl.ds((t ^ flip) * images, images)] = ref[...]


def local(sizes, *arguments):
    (patches, cotangent, mask_rank, mask_count, image_count,
     entry_weight, entry_moment, entry_second, entry_bias, entry_bias_moment, entry_bias_second,
     exit_weight, exit_moment, exit_second, expand_weight, expand_moment, expand_second,
     expand_bias, expand_bias_moment, expand_bias_second, reduce_weight, reduce_moment, reduce_second,
     vectors, vectors_moment, vectors_second, position, position_moment, position_second) = arguments
    n_dp, n_tensor = sizes
    direct = n_dp == 8 and n_tensor == 4
    dp, tensor = lax.axis_index("dp"), lax.axis_index("tensor")
    at = jnp.stack([dp, tensor]).astype(jnp.int32)
    slots, patch_count, width = patches.shape
    images = slots // n_tensor
    pad = -(-patch_count // CHUNK) * CHUNK
    tokens = images * pad
    columns = entry_weight.shape[2]
    hidden = expand_weight.shape[1]
    rows = entry_weight.shape[1]
    heads = columns // HEAD_DIM

    attn_shard = jnp.concatenate(
        [entry_weight[0], entry_weight[1], entry_weight[2], exit_weight.T], 1
    ).astype(HALF)
    expand_shard = expand_weight.astype(HALF)
    reduce_shard = reduce_weight.T.astype(HALF)

    own = lambda array: lax.dynamic_slice_in_dim(array, tensor * images, images, 0)
    masked = (own(mask_rank) < own(mask_count)[:, None]).astype(SINGLE)
    mask = jnp.pad(masked, ((0, 0), (0, pad - patch_count))).reshape(tokens, 1)
    live = (tensor * images + jnp.arange(images, dtype=jnp.int32) < image_count[0]).astype(SINGLE)

    swap = Direct(n_dp, n_tensor)
    if direct:
        part_rows = jnp.concatenate(
            [
                position.astype(HALF),
                jnp.zeros((200 - patch_count, rows), HALF),
                vectors.astype(HALF),
                jnp.zeros((4 * PLACE_ROWS - 207, rows), HALF),
            ]
        )
        block = lax.dynamic_slice_in_dim(part_rows, tensor * PLACE_ROWS, PLACE_ROWS, 0)
        bias_rows = jnp.concatenate(
            [
                expand_bias.astype(HALF),
                jnp.pad(entry_bias[:, 0, :].astype(HALF), ((0, 0), (0, rows - entry_bias.shape[2]))),
                jnp.zeros((SMALL_ROWS - PLACE_ROWS - 3, rows), HALF),
            ]
        )
        small = jnp.pad(jnp.concatenate([block, bias_rows]), ((0, 0), (0, 128 - rows)))
        small = jnp.stack([small] + [swap.along(small, f"z{k}") for k in (1, 2, 3)])
        for name in ("y", "x", "core"):
            small = jnp.concatenate([small, swap.along(small, name)])
        attn_pieces = swap.gather(attn_shard)
        expand_pieces = swap.gather(expand_shard)
        reduce_pieces = swap.gather(reduce_shard)
        layout = swap.grad_layout()
        grad_outs = [shape((4, rows, width), HALF) for _ in layout]
        rows_out = rows
    else:
        def gather(shard):
            whole = lax.all_gather(shard, "dp", axis=0, tiled=True)
            whole = lax.all_gather(whole, "tensor", axis=0)
            turned = [lax.dynamic_index_in_dim(whole, tensor ^ t, 0) for t in range(n_tensor)]
            return [(turned[t], [(t, None)]) for t in range(n_tensor)]

        attn_pieces = gather(attn_shard)
        expand_pieces = gather(expand_shard)
        reduce_pieces = gather(reduce_shard)
        layout = [[(t, None)] for t in range(n_tensor)]
        grad_outs = [shape((1, width, width), HALF) for _ in layout]
        rows_out = width
        everywhere = lambda array, axis: lax.all_gather(array.astype(HALF), "dp", axis=axis, tiled=True)
        place = jnp.pad(everywhere(position, 1), ((0, 256 - patch_count), (0, 0))).astype(SINGLE)
        table_in = jnp.pad(everywhere(vectors, 1), ((0, 1), (0, 0))).astype(SINGLE)
        both = lax.all_gather(everywhere(entry_bias, 2), "tensor", axis=1, tiled=True)
        entry_in = jnp.concatenate([both[0], jnp.zeros_like(both[0]), both[1]], 1)
        entry_in = entry_in.astype(SINGLE)[:, None, :]
        expand_in = lax.all_gather(everywhere(expand_bias, 1), "tensor", axis=0, tiled=True)
        expand_in = expand_in.astype(SINGLE)[:, None, :]

    def pieces_of(pieces):
        return [(piece, ANY) for piece, _ in pieces], [where for _, where in pieces]

    copies = sum(len(where) for where in layout)
    held = pltpu.VMEM((n_tensor, width, width), HALF)
    wide = pltpu.VMEM((tokens, width), SINGLE)
    many = pltpu.SemaphoreType.DMA((copies,))
    one_sem = pltpu.SemaphoreType.DMA
    dense = 2 * tokens * width * width

    small_in = [(small, VMEM)] if direct else [(a, VMEM) for a in (place, table_in, entry_in, expand_in)]
    start_scratch = [pltpu.VMEM((images, patch_count, width), HALF)] * 2
    if direct:
        start_scratch.append(pltpu.VMEM((4 * PLACE_ROWS, width), SINGLE))
    start, normed_one, low, table, entry_shift, expand_shift = kernel_call(
        functools.partial(start_body, images, patch_count, pad, direct),
        [
            (shape((tokens, width), SINGLE), VMEM),
            (shape((tokens, width), HALF), VMEM),
            (shape((tokens, width), HALF), VMEM),
            (shape((8, width), SINGLE), VMEM),
            (shape((n_tensor, 1, 3 * columns), SINGLE), VMEM),
            (shape((n_tensor, 1, hidden), SINGLE), VMEM),
        ],
        [(at, SMEM), (patches, ANY), (cotangent, ANY), (mask, VMEM), (live, SMEM)] + small_in,
        start_scratch + [one_sem((2,))],
        0,
        "start",
    )

    operands, spots = pieces_of(attn_pieces)
    qkv, probs, mixed, attn_full = kernel_call(
        functools.partial(attend_body, images, patch_count, pad, spots),
        [
            (shape((n_tensor, tokens, 3 * columns), HALF), VMEM),
            (shape((n_tensor, images * heads, pad, pad), HALF), VMEM),
            (shape((n_tensor, tokens, columns), HALF), VMEM),
            (shape((n_tensor, width, width), HALF), ANY),
        ],
        [(at, SMEM), (normed_one, VMEM), (entry_shift, VMEM)] + operands,
        [held, many, one_sem],
        6 * dense,
        "attend",
    )

    operands, spots = pieces_of(expand_pieces)
    middle, normed_two, active, slope, expand_full, *grad_reduce = kernel_call(
        functools.partial(up_body, spots, layout, rows_out),
        [
            (shape((tokens, width), SINGLE), VMEM),
            (shape((tokens, width), HALF), VMEM),
            (shape((n_tensor, tokens, hidden), HALF), VMEM),
            (shape((n_tensor, tokens, hidden), HALF), VMEM),
            (shape((n_tensor, width, hidden), HALF), ANY),
        ]
        + [(a, ANY) for a in grad_outs],
        [(at, SMEM)]
        + [(a, VMEM) for a in (start, mixed, attn_full, low, table, expand_shift)]
        + operands,
        [held, wide, held, many, one_sem, many],
        12 * dense,
        "up",
    )

    operands, spots = pieces_of(reduce_pieces)
    grad_upper, reduce_full, sums_expand, *grad_expand = kernel_call(
        functools.partial(down_body, spots, layout, rows_out),
        [
            (shape((n_tensor, tokens, hidden), HALF), VMEM),
            (shape((n_tensor, width, hidden), HALF), ANY),
            (shape((n_tensor, 8, hidden), SINGLE), VMEM),
        ]
        + [(a, ANY) for a in grad_outs],
        [(at, SMEM)] + [(a, VMEM) for a in (low, slope, normed_two)] + operands,
        [held, wide, held, many, one_sem, many],
        10 * dense,
        "down",
    )

    grad_middle, grad_half, grad_mixed, sums_two = kernel_call(
        middle_body,
        [
            (shape((tokens, width), SINGLE), VMEM),
            (shape((tokens, width), HALF), VMEM),
            (shape((n_tensor, tokens, columns), HALF), VMEM),
            (shape((4, 8, width), SINGLE), VMEM),
        ],
        [(a, VMEM) for a in (grad_upper, expand_full, attn_full, middle, low, table)],
        [wide],
        6 * dense,
        "middle",
    )

    grad_qkv, sums_entry, *grad_attn = kernel_call(
        functools.partial(attend_back_body, images, pad, layout, rows_out),
        [
            (shape((n_tensor, tokens, 3 * columns), HALF), VMEM),
            (shape((n_tensor, 8, 3 * columns), SINGLE), VMEM),
        ]
        + [(a, ANY) for a in grad_outs],
        [(at, SMEM)]
        + [(a, VMEM) for a in (qkv, probs, grad_mixed, normed_one, grad_half, mixed)],
        [held, many],
        16 * dense,
        "attend_back",
    )

    (own_out,) = kernel_call(
        functools.partial(output_body, images, patch_count, pad),
        [(shape((images, patch_count, width), HALF), VMEM)],
        [(live, SMEM)] + [(a, VMEM) for a in (middle, active, reduce_full, table)],
        [wide, pltpu.VMEM((tokens, width), HALF)],
        4 * dense,
        "output",
    )

    small_out = (
        [(shape((n_dp * n_tensor, SMALL_ROWS, 128), SINGLE), VMEM)]
        if direct
        else [
            (shape((4 * PLACE_ROWS, width), SINGLE), VMEM),
            (shape((n_tensor, 1, 3 * columns), SINGLE), VMEM),
            (shape((n_tensor, 1, hidden), SINGLE), VMEM),
        ]
    )
    end_scratch = [wide, wide, pltpu.VMEM((tokens, width), HALF)]
    if direct:
        end_scratch.append(pltpu.VMEM((4 * PLACE_ROWS, width), SINGLE))
    own_grad, *small_grads = kernel_call(
        functools.partial(end_body, images, patch_count, pad, direct),
        [(shape((images, patch_count, width), HALF), VMEM)] + small_out,
        [(at, SMEM)]
        + [
            (a, VMEM)
            for a in (grad_qkv, attn_full, start, grad_middle, mask, table, sums_two, sums_entry, sums_expand)
        ],
        end_scratch,
        4 * dense,
        "end",
    )

    def spread(piece):
        far = swap.along(piece, "x")
        near = swap.along(piece, "core")
        return kernel_call(
            functools.partial(place_body, images),
            [(shape(patches.shape, HALF), VMEM)],
            [(at, SMEM)]
            + [(a, VMEM) for a in (piece, near, far, swap.along(far, "core"))],
            [],
            0,
            "spread",
        )[0]

    block_out = spread(own_out)
    patch_grad = spread(own_grad)

    if direct:
        def total(outs):
            parts = swap.reduce(outs)
            return sum(part.astype(SINGLE) for part in parts)

        reduced = total(grad_reduce).T
        expanded = total(grad_expand)
        attn = total(grad_attn)
        (small,) = small_grads
        small = small.astype(HALF)
        for name, count in (("core", 16), ("x", 8), ("y", 4)):
            small = add(small[:count], swap.along(small[count:], name))
        small = sum(
            part.astype(SINGLE)
            for part in [small[0]] + [swap.along(small[k], f"z{k}") for k in (1, 2, 3)]
        )
        pair = jnp.stack([small, swap.along(small, "core")])
        four = jnp.concatenate([pair, swap.along(pair, "x")])
        four = [lax.dynamic_index_in_dim(four, tensor ^ t, 0, keepdims=False) for t in range(n_tensor)]
        spot = jnp.concatenate([part[:PLACE_ROWS, :rows] for part in four])
        grad_place = spot[:patch_count]
        grad_table = spot[200:207]
        grad_expand_shift = small[PLACE_ROWS : PLACE_ROWS + 1, :rows]
        grad_entry_shift = small[PLACE_ROWS + 1 : PLACE_ROWS + 3, : entry_bias.shape[2]][:, None, :]
    else:
        def total(outs):
            turned = jnp.concatenate([out.astype(SINGLE) for out in outs])
            turned = jnp.concatenate(
                [lax.dynamic_index_in_dim(turned, tensor ^ t, 0) for t in range(n_tensor)]
            )
            mine = lax.psum_scatter(turned, "tensor", scatter_dimension=0, tiled=True)[0]
            return lax.psum_scatter(mine, "dp", scatter_dimension=0, tiled=True)

        reduced = total(grad_reduce).T
        expanded = total(grad_expand)
        attn = total(grad_attn)
        spot, entry_part, expand_part = small_grads
        spot = lax.psum(lax.psum_scatter(spot, "dp", scatter_dimension=1, tiled=True), "tensor")
        grad_place = spot[:patch_count]
        grad_table = spot[200:207]
        share = lambda array, axis: lax.psum_scatter(
            lax.psum_scatter(array, "tensor", scatter_dimension=0, tiled=True)[0],
            "dp",
            scatter_dimension=axis,
            tiled=True,
        )
        grad_expand_shift = share(expand_part, 1)
        ends = [share(entry_part[:, :, first : first + columns], 1) for first in (0, 2 * columns)]
        grad_entry_shift = jnp.stack(ends)

    grad_entry = jnp.stack([attn[:, j * columns : (j + 1) * columns] for j in range(3)])
    grad_exit = attn[:, 3 * columns :].T

    entry = adamw(entry_weight, entry_moment, entry_second, grad_entry, 0.05, 0.05)
    entry_b = adamw(entry_bias, entry_bias_moment, entry_bias_second, grad_entry_shift, 0.3, 0.0)
    exits = adamw(exit_weight, exit_moment, exit_second, grad_exit, 0.05, 0.05)
    expand = adamw(expand_weight, expand_moment, expand_second, expanded, 0.05, 0.05)
    expand_b = adamw(expand_bias, expand_bias_moment, expand_bias_second, grad_expand_shift, 0.3, 0.0)
    reduce_w = adamw(reduce_weight, reduce_moment, reduce_second, reduced, 0.05, 0.05)
    table_new = adamw(vectors, vectors_moment, vectors_second, grad_table, 0.3, 0.0)
    place_new = adamw(position, position_moment, position_second, grad_place, 0.1, 0.0)
    return (block_out, patch_grad, *entry, *entry_b, *exits, *expand, *expand_b, *reduce_w, *table_new, *place_new)


def solution(mesh):
    images = P("dp", None, None)
    entry = P(None, "dp", "tensor")
    entry_bias = P(None, "tensor", "dp")
    outer = P("tensor", "dp")
    expand = P("dp", "tensor")
    table = P(None, "dp")
    weights = (entry, entry_bias, outer, expand, outer, outer, table, table)
    placed = (images, images, P("dp", None), P("dp"), P("dp"))
    placed += tuple(spec for spec in weights for _ in range(3))
    given = (images, images) + tuple(spec for spec in weights for _ in range(4))
    sizes = (mesh.shape["dp"], mesh.shape["tensor"])
    return jax.shard_map(
        functools.partial(local, sizes),
        mesh=mesh,
        in_specs=placed,
        out_specs=given,
        check_vma=False,
    )
```

```python
import functools

import jax
import jax.numpy as jnp
from jax import lax
from jax.experimental import pallas as pl
from jax.experimental.pallas import tpu as pltpu
from jax.sharding import PartitionSpec as P

HEAD_DIM = 64
STEP = 7
NORM_EPS = 1e-06
HALF = jnp.bfloat16
SINGLE = jnp.float32
VMEM = pl.BlockSpec(memory_space=pltpu.VMEM)
SMEM = pl.BlockSpec(memory_space=pltpu.SMEM)
ANY = pl.BlockSpec(memory_space=pl.ANY)
CHUNK = 16
COST = 0.001
SMALL_ROWS = 80
PLACE_ROWS = 64


def adamw(master, moment, second, grad, rate, decay):
    moment = 0.9 * moment + 0.1 * grad
    second = 0.999 * second + 0.001 * grad * grad
    fixed_first = moment / (1.0 - 0.9**STEP)
    fixed_second = second / (1.0 - 0.999**STEP)
    master = master - rate * (fixed_first / (jnp.sqrt(fixed_second) + 1e-08) + decay * master)
    return (master, moment, second, master.astype(jnp.bfloat16))


def dot(left, right):
    return jnp.dot(left, right, preferred_element_type=SINGLE)


def row_dot(left, right):
    return lax.dot_general(left, right, (((1,), (1,)), ((), ())), preferred_element_type=SINGLE)


def column_dot(left, right):
    return lax.dot_general(left, right, (((0,), (0,)), ((), ())), preferred_element_type=SINGLE)


def kernel_call(body, outs, operands, scratch, microseconds, name):
    flops = int(microseconds * 1e9 * COST)
    moved = 1024
    return pl.pallas_call(
        body,
        out_shape=[a for a, _ in outs],
        in_specs=[spec for _, spec in operands],
        out_specs=[spec for _, spec in outs],
        scratch_shapes=scratch,
        cost_estimate=pl.CostEstimate(flops=flops, bytes_accessed=moved, transcendentals=0),
        name=name,
    )(*[a for a, _ in operands])


def shape(dims, kind):
    return jax.ShapeDtypeStruct(dims, kind)


def add(*parts):
    total = parts[0].astype(SINGLE)
    for part in parts[1:]:
        total = total + part.astype(SINGLE)
    return total.astype(HALF)


def after(value, *others):
    return lax.optimization_barrier((value, *others))[0]


class Swap:
    def __init__(self, n_dp, n_tensor):
        self.n_dp = n_dp
        self.n_tensor = n_tensor

    def flip(self, array, axis, bits):
        count = self.n_dp if axis == "dp" else self.n_tensor
        return lax.ppermute(array, axis, [(i, i ^ bits) for i in range(count)])

    def along(self, array, name):
        axis, bits = {
            "core": ("tensor", 1),
            "x": ("tensor", 2),
            "y": ("dp", 1),
            "z1": ("dp", 2),
            "z2": ("dp", 4),
            "z3": ("dp", 6),
        }[name]
        return self.flip(array, axis, bits)

    def gather_line(self, shard):
        first = jnp.stack([shard, self.along(shard, "z2")])
        return first, self.along(first, "z1")

    def gather_plane(self, first, last):
        first = jnp.concatenate([first, self.along(first, "y")])
        last = jnp.concatenate([last, self.along(last, "x")])
        first_x = self.along(first, "x")
        last_y = self.along(last, "y")
        return [
            (first, [(0, 0), (0, 4), (0, 1), (0, 5)]),
            (first_x, [(1, 0), (1, 4), (1, 1), (1, 5)]),
            (last, [(0, 2), (0, 6), (1, 2), (1, 6)]),
            (last_y, [(0, 3), (0, 7), (1, 3), (1, 7)]),
        ]

    def plane_first(self, shard):
        pair = jnp.stack([shard, self.along(shard, "x")])
        return jnp.concatenate([pair, self.along(pair, "y")])

    def line_last(self, four):
        eight = jnp.concatenate([four, self.along(four, "z2")])
        spots = lambda k: [(x, 2 * k + y) for y in (0, 1) for x in (0, 1)]
        return [(eight, spots(0) + spots(2)), (self.along(eight, "z1"), spots(1) + spots(3))]

    def grad_layout(self):
        layout = []
        for half, steps in enumerate(((0, 2), (1, 3))):
            for first in (0, 1):
                blocks = []
                for second in (0, 1):
                    x, y = (first, second) if half == 0 else (second, first)
                    for k in steps:
                        blocks.append((x, 2 * k + y))
                layout.append(blocks)
        return layout

    def reduce(self, outs):
        came_a = self.along(outs[1], "x")
        came_b = self.along(outs[3], "y")
        far_b = self.along(add(outs[2][2:], came_b[2:]), "x")
        far_a = self.along(add(outs[0][2:], came_a[2:]), "y")
        over = self.along(add(outs[2][:2], came_b[:2], far_b), "z1")
        parts = (outs[0], came_a, far_a, over)
        there = self.along(add(*[part[1] for part in parts]), "z2")
        return [part[0] for part in parts] + [there]

    def grad_layout_line(self):
        spots = lambda k: [(x, 2 * k + y) for y in (0, 1) for x in (0, 1)]
        return [spots(0), spots(2), spots(1) + spots(3)]

    def reduce_line(self, outs):
        came = self.along(outs[2], "z1")
        there = self.along(add(outs[1], came[4:]), "z2")
        parts = (outs[0], came[:4], there)
        over = self.along(add(*[part[2:] for part in parts]), "y")
        parts = (*parts, over)
        last = self.along(add(*[part[1] for part in parts]), "x")
        return [part[0] for part in parts] + [last]


def load_pieces(place_ref, piece_refs, spots, dst_ref, sems):
    copies = []
    for ref, where in zip(piece_refs, spots):
        for j, (pair_flip, dp_flip) in enumerate(where):
            if dp_flip is None:
                dst = dst_ref.at[pair_flip]
            else:
                rows = ref.shape[1]
                row = pl.multiple_of((place_ref[0] ^ dp_flip) * rows, rows)
                dst = dst_ref.at[pair_flip, pl.ds(row, rows), :]
            copies.append(pltpu.make_async_copy(ref.at[j], dst, sems.at[len(copies)]))
    for copy in copies:
        copy.start()
    return copies


def store_grads(place_ref, src_ref, out_refs, layout, rows, sems):
    copies = []
    for ref, where in zip(out_refs, layout):
        for j, (pair_flip, dp_flip) in enumerate(where):
            if dp_flip is None:
                src = src_ref.at[pair_flip]
            else:
                row = pl.multiple_of((place_ref[0] ^ dp_flip) * rows, rows)
                src = src_ref.at[pair_flip, pl.ds(row, rows), :]
            copies.append(pltpu.make_async_copy(src, ref.at[j], sems.at[len(copies)]))
    for copy in copies:
        copy.start()
    return copies


def wait_all(copies):
    for copy in copies:
        copy.wait()


def fold(rows):
    return rows[:8] + rows[8:]


def norm_scaled(rows):
    scale = 1.0 / rows.shape[-1]
    centered = rows - jnp.sum(rows, -1, keepdims=True) * scale
    inverse = lax.rsqrt(jnp.sum(centered * centered, -1, keepdims=True) * scale + NORM_EPS)
    return centered * inverse, inverse


def norm_grad(grad, scaled, inverse, gain):
    scale = 1.0 / grad.shape[-1]
    e = grad * gain
    mean_e = jnp.sum(e, -1, keepdims=True) * scale
    mean_cross = jnp.sum(e * scaled, -1, keepdims=True) * scale
    return inverse * (e - mean_e - scaled * mean_cross)


def over_rows(tokens, body, init):
    def one(j, carry):
        return body(pl.ds(pl.multiple_of(j * CHUNK, CHUNK), CHUNK), carry)

    return lax.fori_loop(0, tokens // CHUNK, one, init)


def small_slot(place_ref, t_at, dp_at):
    t_flip = place_ref[1] ^ t_at
    dp_flip = place_ref[0] ^ dp_at
    return (t_flip & 1) * 16 + (t_flip >> 1) * 8 + (dp_flip & 1) * 4 + (dp_flip >> 1)


def start_body(images, patches, pad, packed, place_ref, patch_ref, cot_ref, mask_ref, live_ref, *rest):
    if packed:
        (small_ref, start_ref, normed_ref, low_ref, table_ref, entry_ref, expand_ref, pair, both, spot, sems) = rest
    else:
        (spot, table_in, entry_in, expand_in, start_ref, normed_ref, low_ref, table_ref, entry_ref, expand_ref, pair, both, sems) = rest
    first = (place_ref[1] >> 1) * images
    copies = [
        pltpu.make_async_copy(patch_ref.at[pl.ds(first, images)], pair, sems.at[0]),
        pltpu.make_async_copy(cot_ref.at[pl.ds(first, images)], both, sems.at[1]),
    ]
    for copy in copies:
        copy.start()
    n_tensor = entry_ref.shape[0]
    columns = entry_ref.shape[2] // 3
    entry_ref[...] = jnp.zeros_like(entry_ref)
    if packed:
        n_dp = small_ref.shape[0] // n_tensor
        part = spot.shape[1] // n_dp
        own = part // n_tensor
        for dp_at in range(n_dp):
            for t_at in range(n_tensor):
                block = small_ref[small_slot(place_ref, t_at, dp_at)].astype(SINGLE)
                spot[PLACE_ROWS * t_at : PLACE_ROWS * (t_at + 1), part * dp_at : part * (dp_at + 1)] = block[:PLACE_ROWS, :part]
                bias = block[PLACE_ROWS : PLACE_ROWS + 8]
                expand_ref[t_at, :, part * dp_at : part * (dp_at + 1)] = bias[0:1, :part]
                entry_ref[t_at, :, own * dp_at : own * (dp_at + 1)] = bias[1:2, :own]
                entry_ref[t_at, :, 2 * columns + own * dp_at : 2 * columns + own * (dp_at + 1)] = bias[2:3, :own]
        table_ref[...] = spot[200:208, :]
    else:
        table_ref[...] = table_in[...]
        entry_ref[...] = entry_in[...]
        expand_ref[...] = expand_in[...]
    wait_all(copies)
    token = table_ref[6:7, :]
    empty = jnp.zeros((CHUNK, start_ref.shape[1]), SINGLE)
    for i in range(images):
        start_ref[(i + 1) * pad - CHUNK : (i + 1) * pad, :] = empty
        low_ref[(i + 1) * pad - CHUNK : (i + 1) * pad, :] = empty.astype(HALF)
        rows = pl.ds(i * pad, patches)
        picked = jnp.where(mask_ref[rows, :] > 0.5, token, pair[i].astype(SINGLE))
        start_ref[rows, :] = picked + spot[:patches, :]
        low_ref[rows, :] = (both[i].astype(SINGLE) * live_ref[i]).astype(HALF)
    gain, shift = table_ref[0:1, :], table_ref[1:2, :]

    def one(rows, carry):
        scaled, _ = norm_scaled(start_ref[rows, :])
        normed_ref[rows, :] = (scaled * gain + shift).astype(HALF)
        return carry

    over_rows(start_ref.shape[0], one, 0)


def attend_body(images, patches, pad, spots, place_ref, normed_ref, bias_ref, *rest):
    n = len(spots)
    piece_refs = rest[:n]
    qkv_ref, probs_ref, mixed_ref, branch_ref, full_ref, held, total, sems, out_sem = rest[n:]
    columns = mixed_ref.shape[2]
    heads = columns // HEAD_DIM
    wait_all(load_pieces(place_ref, piece_refs, spots, held, sems))
    out = pltpu.make_async_copy(held, full_ref, out_sem)
    out.start()
    lanes = lax.broadcasted_iota(jnp.int32, (pad, pad), 1)

    for b in range(held.shape[0]):
        qkv = dot(normed_ref[...], held[b, :, : 3 * columns]) + bias_ref[place_ref[1] ^ (2 * b)]
        qkv_ref[b] = qkv.astype(HALF)

        def one(i, carry):
            rows = pl.ds(pl.multiple_of(i * pad, CHUNK), pad)
            for h in range(heads):
                at = h * HEAD_DIM
                query = qkv_ref[b, rows, at : at + HEAD_DIM]
                keys = qkv_ref[b, rows, columns + at : columns + at + HEAD_DIM]
                values = qkv_ref[b, rows, 2 * columns + at : 2 * columns + at + HEAD_DIM]
                scores = row_dot(query, keys) * HEAD_DIM ** (-0.5)
                scores = jnp.where(lanes < patches, scores, -1e30)
                risen = jnp.exp(scores - jnp.max(scores, -1, keepdims=True))
                probs = (risen * (1.0 / jnp.sum(risen, -1, keepdims=True))).astype(HALF)
                probs_ref[b, i * heads + h] = probs
                mixed_ref[b, rows, at : at + HEAD_DIM] = dot(probs, values).astype(HALF)
            return carry

        lax.fori_loop(0, images, one, 0)
        part = row_dot(mixed_ref[b], held[b, :, 3 * columns :])
        if b == 0:
            total[...] = part
        elif b < held.shape[0] - 1:
            total[...] += part
        else:
            branch_ref[...] = (total[...] + part).astype(HALF)
    out.wait()


def up_body(spots, layout, rows_out, place_ref, start_ref, branch_ref, came_ref, low_ref, table_ref, bias_ref, *rest):
    n, m = len(spots), len(layout)
    piece_refs = rest[:n]
    middle_ref, normed_ref, active_ref, slope_ref, expand_ref = rest[n : n + 5]
    out_refs = rest[n + 5 : n + 5 + m]
    held, upper, grads, sems, out_sem, grad_sems = rest[n + 5 + m :]
    tokens = start_ref.shape[0]
    copies = load_pieces(place_ref, piece_refs, spots, held, sems)
    gain, shift, bias = table_ref[2:3, :], table_ref[3:4, :], table_ref[4:5, :]

    def one(rows, carry):
        branch = branch_ref[rows, :].astype(SINGLE) + came_ref[rows, :].astype(SINGLE)
        middle = start_ref[rows, :] + branch + bias
        middle_ref[rows, :] = middle
        scaled, _ = norm_scaled(middle)
        normed_ref[rows, :] = (scaled * gain + shift).astype(HALF)
        return carry

    over_rows(tokens, one, 0)
    wait_all(copies)
    out = pltpu.make_async_copy(held, expand_ref, out_sem)
    out.start()

    def up(b, carry):
        upper[...] = dot(normed_ref[...], held[b]) + bias_ref[place_ref[1] ^ (2 * b)]

        def bend(rows, inner):
            u = upper[rows, :]
            cdf = 0.5 * (1.0 + lax.erf(u * 0.7071067811865476))
            active_ref[b, rows, :] = (u * cdf).astype(HALF)
            slope = cdf + u * (jnp.exp(u * u * -0.5) * 0.3989422804014327)
            slope_ref[b, rows, :] = slope.astype(HALF)
            return inner

        over_rows(tokens, bend, 0)
        grads[b] = column_dot(low_ref[...], active_ref[b]).astype(HALF)
        return carry

    lax.fori_loop(0, held.shape[0], up, 0)
    wait_all(store_grads(place_ref, grads, out_refs, layout, rows_out, grad_sems))
    out.wait()


def down_body(spots, place_ref, low_ref, slope_ref, expand_ref, *rest):
    n = len(spots)
    piece_refs = rest[:n]
    grad_upper_ref, normed_grad_ref, reduce_ref, sums_ref, held, upper, total, sems, out_sem = rest[n:]
    tokens = low_ref.shape[0]
    wait_all(load_pieces(place_ref, piece_refs, spots, held, sems))
    out = pltpu.make_async_copy(held, reduce_ref, out_sem)
    out.start()
    for b in range(held.shape[0]):
        upper[...] = dot(low_ref[...], held[b])

        def bend(rows, sums):
            grad = (upper[rows, :] * slope_ref[b, rows, :].astype(SINGLE)).astype(HALF)
            grad_upper_ref[b, rows, :] = grad
            return sums + fold(grad.astype(SINGLE))

        sums_ref[b] = over_rows(tokens, bend, jnp.zeros((8, upper.shape[1]), SINGLE))
        part = row_dot(grad_upper_ref[b], expand_ref[b])
        if b == 0:
            total[...] = part
        elif b < held.shape[0] - 1:
            total[...] += part
        else:
            normed_grad_ref[...] = (total[...] + part).astype(HALF)
    out.wait()


def expand_body(layout, rows_out, place_ref, normed_ref, grad_upper_ref, *rest):
    out_refs = rest[: len(layout)]
    grads, grad_sems = rest[len(layout) :]

    def one(b, carry):
        grads[b] = column_dot(normed_ref[...], grad_upper_ref[b]).astype(HALF)
        return carry

    lax.fori_loop(0, grads.shape[0], one, 0)
    wait_all(store_grads(place_ref, grads, out_refs, layout, rows_out, grad_sems))


def back_body(images, pad, layout, rows_out, place_ref, normed_grad_ref, came_ref, middle_ref, low_ref, table_ref, full_ref, qkv_ref, probs_ref, normed_ref, mixed_ref, *rest):
    m = len(layout)
    grad_middle_ref, grad_qkv_ref, sums_two_ref, sums_entry_ref = rest[:4]
    out_refs = rest[4 : 4 + m]
    half, grad_mixed, grads, grad_sems = rest[4 + m :]
    blocks, tokens, columns = mixed_ref.shape
    heads = columns // HEAD_DIM
    scale = HEAD_DIM ** (-0.5)
    gain = table_ref[2:3, :]

    def one(rows, carry):
        scaled, inverse = norm_scaled(middle_ref[rows, :])
        grad = normed_grad_ref[rows, :].astype(SINGLE) + came_ref[rows, :].astype(SINGLE)
        low = low_ref[rows, :].astype(SINGLE)
        out = low + norm_grad(grad, scaled, inverse, gain)
        grad_middle_ref[rows, :] = out
        half[rows, :] = out.astype(HALF)
        parts = (grad * scaled, grad, out, low)
        return tuple(c + fold(p) for c, p in zip(carry, parts))

    zero = jnp.zeros((8, low_ref.shape[1]), SINGLE)
    totals = over_rows(tokens, one, (zero,) * 4)
    for row, total in enumerate(totals):
        sums_two_ref[row] = total

    for b in range(blocks):
        grad_mixed[...] = dot(half[...], full_ref[b, :, 3 * columns :]).astype(HALF)

        def attend(i, carry):
            rows = pl.ds(pl.multiple_of(i * pad, CHUNK), pad)
            for h in range(heads):
                at = h * HEAD_DIM
                query = qkv_ref[b, rows, at : at + HEAD_DIM]
                keys = qkv_ref[b, rows, columns + at : columns + at + HEAD_DIM]
                values = qkv_ref[b, rows, 2 * columns + at : 2 * columns + at + HEAD_DIM]
                grad = grad_mixed[rows, at : at + HEAD_DIM]
                low = probs_ref[b, i * heads + h]
                probs = low.astype(SINGLE)
                grad_qkv_ref[b, rows, 2 * columns + at : 2 * columns + at + HEAD_DIM] = column_dot(low, grad).astype(HALF)
                grad_probs = row_dot(grad, values)
                inner = jnp.sum(probs * grad_probs, -1, keepdims=True)
                grad_scores = (probs * (grad_probs - inner)).astype(HALF)
                grad_qkv_ref[b, rows, at : at + HEAD_DIM] = (dot(grad_scores, keys) * scale).astype(HALF)
                grad_qkv_ref[b, rows, columns + at : columns + at + HEAD_DIM] = (column_dot(grad_scores, query) * scale).astype(HALF)
            return carry

        lax.fori_loop(0, images, attend, 0)
        grads[b, :, : 3 * columns] = column_dot(normed_ref[...], grad_qkv_ref[b]).astype(HALF)
        grads[b, :, 3 * columns :] = column_dot(half[...], mixed_ref[b]).astype(HALF)

        def sums(rows, total):
            return total + fold(grad_qkv_ref[b, rows, :].astype(SINGLE))

        sums_entry_ref[b] = over_rows(tokens, sums, jnp.zeros((8, 3 * columns), SINGLE))
    wait_all(store_grads(place_ref, grads, out_refs, layout, rows_out, grad_sems))


def normed_body(place_ref, grad_qkv_ref, full_ref, keep_ref, send_ref, total):
    blocks = grad_qkv_ref.shape[0]
    width = grad_qkv_ref.shape[2]
    total[...] = row_dot(grad_qkv_ref[0], full_ref[0, :, :width])
    for b in range(1, blocks):
        total[...] += row_dot(grad_qkv_ref[b], full_ref[b, :, :width])
    count = keep_ref.shape[0]
    core = place_ref[1] & 1
    keep_ref[...] = total[pl.ds(pl.multiple_of(core * count, count), count), :]
    send_ref[...] = total[pl.ds(pl.multiple_of((1 - core) * count, count), count), :].astype(HALF)


def output_body(place_ref, middle_ref, active_ref, reduce_ref, table_ref, keep_ref, send_ref, total):
    total[...] = row_dot(active_ref[0], reduce_ref[0])
    for b in range(1, active_ref.shape[0]):
        total[...] += row_dot(active_ref[b], reduce_ref[b])
    count = keep_ref.shape[0]
    core = place_ref[1] & 1
    rows = pl.ds(pl.multiple_of(core * count, count), count)
    keep_ref[...] = total[rows, :] + middle_ref[rows, :] + table_ref[5:6, :]
    send_ref[...] = total[pl.ds(pl.multiple_of((1 - core) * count, count), count), :].astype(HALF)


def end_body(images, patches, pad, packed, place_ref, keep_ref, came_ref, start_ref, grad_middle_ref, mask_ref, table_ref, sums_two_ref, sums_entry_ref, sums_expand_ref, *rest):
    if packed:
        out_ref, small_ref, ended, spot = rest
    else:
        out_ref, spot, entry_ref, expand_ref, ended = rest
    count, width = keep_ref.shape
    columns = sums_entry_ref.shape[2] // 3
    blocks = sums_entry_ref.shape[0]
    core = place_ref[1] & 1
    gain = table_ref[0:1, :]

    def one(j, carry):
        rows = pl.ds(pl.multiple_of(j * CHUNK, CHUNK), CHUNK)
        far = pl.ds(pl.multiple_of(core * count + j * CHUNK, CHUNK), CHUNK)
        scaled, inverse = norm_scaled(start_ref[far, :])
        grad = keep_ref[rows, :] + came_ref[rows, :].astype(SINGLE)
        out = grad_middle_ref[far, :] + norm_grad(grad, scaled, inverse, gain)
        ended[rows, :] = out
        masked = mask_ref[far, :] > 0.5
        out_ref[rows, :] = jnp.where(masked, 0.0, out).astype(HALF)
        parts = (grad * scaled, grad, jnp.where(masked, out, 0.0))
        return tuple(c + fold(p) for c, p in zip(carry, parts))

    zero = jnp.zeros((8, width), SINGLE)
    totals = lax.fori_loop(0, count // CHUNK, one, (zero,) * 3)
    place = ended[:pad, :]
    for i in range(1, images):
        place = place + ended[i * pad : (i + 1) * pad, :]
    column = lambda total: jnp.sum(total, 0, keepdims=True)
    spot[...] = jnp.zeros_like(spot)
    spot[:pad, :] = place
    once = jnp.where(core == 0, 1.0, 0.0)
    rows = [column(totals[0]), column(totals[1])]
    rows += [column(sums_two_ref[row]) * once for row in range(4)]
    rows += [column(totals[2])]
    for row, total in enumerate(rows):
        spot[200 + row : 201 + row, :] = total
    if not packed:
        entry_ref[...] = jnp.zeros_like(entry_ref)
        expand_ref[...] = jnp.zeros_like(expand_ref)
        for b in range(blocks):
            entry_ref[place_ref[1] ^ (2 * b)] = column(sums_entry_ref[b])
            expand_ref[place_ref[1] ^ (2 * b)] = column(sums_expand_ref[b])
        return
    n_tensor = 2 * blocks
    n_dp = small_ref.shape[0] // n_tensor
    part = width // n_dp
    own = part // n_tensor
    small_ref[...] = jnp.zeros_like(small_ref)
    for dp_at in range(n_dp):
        for t_at in range(n_tensor):
            slot = small_slot(place_ref, t_at, dp_at)
            block = spot[PLACE_ROWS * t_at : PLACE_ROWS * (t_at + 1), part * dp_at : part * (dp_at + 1)]
            small_ref[slot, :PLACE_ROWS, :part] = block.astype(HALF)
        for b in range(blocks):
            dp_flip = place_ref[0] ^ dp_at
            slot = b * 8 + (dp_flip & 1) * 4 + (dp_flip >> 1)
            entry = column(sums_entry_ref[b])
            expand = column(sums_expand_ref[b])
            wide = expand[:, part * dp_at : part * (dp_at + 1)]
            short = entry[:, own * dp_at : own * (dp_at + 1)]
            shorter = entry[:, 2 * columns + own * dp_at : 2 * columns + own * (dp_at + 1)]
            fill = lambda row: jnp.concatenate([row, jnp.zeros((1, 128 - row.shape[1]), SINGLE)], 1)
            tall = jnp.concatenate([fill(wide), fill(short), fill(shorter), jnp.zeros((CHUNK - 3, 128), SINGLE)], 0)
            small_ref[slot, PLACE_ROWS:, :] = tall.astype(HALF)


def place_body(images, patches, pad, place_ref, own_ref, core_ref, x_ref, far_ref, out_ref):
    for flip, ref in enumerate((own_ref, core_ref, x_ref, far_ref)):
        for i in range(images):
            out_ref[(place_ref[1] ^ flip) * images + i] = ref[i * pad : i * pad + patches, :]


def local(sizes, *arguments):
    (patches, cotangent, mask_rank, mask_count, image_count,
     entry_weight, entry_moment, entry_second, entry_bias, entry_bias_moment, entry_bias_second,
     exit_weight, exit_moment, exit_second, expand_weight, expand_moment, expand_second,
     expand_bias, expand_bias_moment, expand_bias_second, reduce_weight, reduce_moment, reduce_second,
     vectors, vectors_moment, vectors_second, position, position_moment, position_second) = arguments
    n_dp, n_tensor = sizes
    blocks = n_tensor // 2
    direct = n_dp == 8 and n_tensor == 4
    dp, tensor = lax.axis_index("dp"), lax.axis_index("tensor")
    at = jnp.stack([dp, tensor]).astype(jnp.int32)
    slots, patch_count, width = patches.shape
    images = slots // blocks
    share = images // 2
    pad = -(-patch_count // CHUNK) * CHUNK
    tokens = images * pad
    columns = entry_weight.shape[2]
    hidden = expand_weight.shape[1]
    rows = entry_weight.shape[1]
    heads = columns // HEAD_DIM
    swap = Swap(n_dp, n_tensor)

    attn_shard = jnp.concatenate(
        [entry_weight[0], entry_weight[1], entry_weight[2], exit_weight.T], 1
    ).astype(HALF)
    expand_shard = expand_weight.astype(HALF)
    reduce_shard = reduce_weight.T.astype(HALF)

    first_image = (tensor // 2) * images
    own = lambda array: lax.dynamic_slice_in_dim(array, first_image, images, 0)
    masked = (own(mask_rank) < own(mask_count)[:, None]).astype(SINGLE)
    mask = jnp.pad(masked, ((0, 0), (0, pad - patch_count))).reshape(tokens, 1)
    live = (first_image + jnp.arange(images, dtype=jnp.int32) < image_count[0]).astype(SINGLE)

    if direct:
        part_rows = jnp.concatenate(
            [
                position.astype(HALF),
                jnp.zeros((200 - patch_count, rows), HALF),
                vectors.astype(HALF),
                jnp.zeros((4 * PLACE_ROWS - 207, rows), HALF),
            ]
        )
        block = lax.dynamic_slice_in_dim(part_rows, tensor * PLACE_ROWS, PLACE_ROWS, 0)
        bias_rows = jnp.concatenate(
            [
                expand_bias.astype(HALF),
                jnp.pad(entry_bias[:, 0, :].astype(HALF), ((0, 0), (0, rows - entry_bias.shape[2]))),
                jnp.zeros((SMALL_ROWS - PLACE_ROWS - 3, rows), HALF),
            ]
        )
        small = jnp.pad(jnp.concatenate([block, bias_rows]), ((0, 0), (0, 128 - rows)))
        attn_line = swap.gather_line(attn_shard)
        small = jnp.stack([small] + [swap.along(small, f"z{k}") for k in (1, 2, 3)])
        for name in ("y", "x", "core"):
            small = jnp.concatenate([small, swap.along(small, name)])
        reduce_plane = swap.plane_first(reduce_shard)
        expand_line = swap.gather_line(after(expand_shard, *attn_line))
        attn_pieces = swap.gather_plane(*attn_line)
        reduce_pieces = swap.line_last(after(reduce_plane, *expand_line))
        arrived = [attn_pieces[1][0], attn_pieces[3][0]]
        expand_line = lax.optimization_barrier((*expand_line, *arrived))
        expand_pieces = swap.gather_plane(*expand_line[:2])
        layout = swap.grad_layout()
        layout_line = swap.grad_layout_line()
        grad_outs = [shape((len(where), rows, width), HALF) for where in layout]
        grad_outs_line = [shape((len(where), rows, width), HALF) for where in layout_line]
        rows_out = rows
    else:
        def gather(shard):
            whole = lax.all_gather(shard, "dp", axis=0, tiled=True)
            return [
                ((swap.flip(whole, "tensor", 2 * b) if b else whole)[None], [(b, None)])
                for b in range(blocks)
            ]

        attn_pieces = gather(attn_shard)
        expand_pieces = gather(expand_shard)
        reduce_pieces = gather(reduce_shard)
        layout = layout_line = [[(b, None)] for b in range(blocks)]
        grad_outs = grad_outs_line = [shape((1, width, width), HALF) for _ in layout]
        rows_out = width
        everywhere = lambda array, axis: lax.all_gather(array.astype(HALF), "dp", axis=axis, tiled=True)
        place = jnp.pad(everywhere(position, 1), ((0, 256 - patch_count), (0, 0))).astype(SINGLE)
        table_in = jnp.pad(everywhere(vectors, 1), ((0, 1), (0, 0))).astype(SINGLE)
        both = lax.all_gather(everywhere(entry_bias, 2), "tensor", axis=1, tiled=True)
        entry_in = jnp.concatenate([both[0], jnp.zeros_like(both[0]), both[1]], 1)
        entry_in = entry_in.astype(SINGLE)[:, None, :]
        expand_in = lax.all_gather(everywhere(expand_bias, 1), "tensor", axis=0, tiled=True)
        expand_in = expand_in.astype(SINGLE)[:, None, :]

    def pieces_of(pieces):
        return [(piece, ANY) for piece, _ in pieces], [where for _, where in pieces]

    held = pltpu.VMEM((blocks, width, width), HALF)
    wide = pltpu.VMEM((tokens, width), SINGLE)
    sem = pltpu.SemaphoreType.DMA
    many = sem((8 * blocks,))
    whole_half = (shape((tokens, width), HALF), VMEM)
    whole_single = (shape((tokens, width), SINGLE), VMEM)
    share_half = (shape((share * pad, width), HALF), VMEM)
    share_single = (shape((share * pad, width), SINGLE), VMEM)
    hidden_half = (shape((blocks, tokens, hidden), HALF), VMEM)
    weight = (shape((blocks, width, hidden), HALF), ANY)
    qkv_half = (shape((blocks, tokens, 3 * columns), HALF), VMEM)
    at_in = [(at, SMEM)]

    small_in = [small] if direct else [place, table_in, entry_in, expand_in]
    start_scratch = [pltpu.VMEM((images, patch_count, width), HALF)] * 2
    if direct:
        start_scratch.append(pltpu.VMEM((4 * PLACE_ROWS, width), SINGLE))
    start, normed_one, low, table, entry_shift, expand_shift = kernel_call(
        functools.partial(start_body, images, patch_count, pad, direct),
        [
            whole_single,
            whole_half,
            whole_half,
            (shape((8, width), SINGLE), VMEM),
            (shape((n_tensor, 1, 3 * columns), SINGLE), VMEM),
            (shape((n_tensor, 1, hidden), SINGLE), VMEM),
        ],
        at_in
        + [(patches, ANY), (cotangent, ANY), (mask, VMEM), (live, SMEM)]
        + [(a, VMEM) for a in small_in],
        start_scratch + [sem((2,))],
        10,
        "start",
    )

    operands, spots = pieces_of(attn_pieces)
    qkv, probs, mixed, branch, attn_full = kernel_call(
        functools.partial(attend_body, images, patch_count, pad, spots),
        [
            qkv_half,
            (shape((blocks, images * heads, pad, pad), HALF), VMEM),
            (shape((blocks, tokens, columns), HALF), VMEM),
            whole_half,
            weight,
        ],
        at_in
        + [(after(normed_one, reduce_pieces[0][0]), VMEM), (entry_shift, VMEM)]
        + operands,
        [held, wide, many, sem],
        16,
        "attend",
    )
    branch_came = swap.along(branch, "core")

    operands, spots = pieces_of(expand_pieces)
    middle, normed_two, active, slope, expand_full, *grad_reduce = kernel_call(
        functools.partial(up_body, spots, layout_line, rows_out),
        [whole_single, whole_half, hidden_half, hidden_half, weight]
        + [(a, ANY) for a in grad_outs_line],
        at_in
        + [(a, VMEM) for a in (start, branch, branch_came, low, table, expand_shift)]
        + operands,
        [held, wide, held, many, sem, many],
        22,
        "up",
    )

    operands, spots = pieces_of(reduce_pieces)
    grad_upper, normed_grad, reduce_full, sums_expand = kernel_call(
        functools.partial(down_body, spots),
        [hidden_half, whole_half, weight, (shape((blocks, 8, hidden), SINGLE), VMEM)],
        at_in + [(a, VMEM) for a in (low, slope, expand_full)] + operands,
        [held, wide, wide, many, sem],
        12,
        "down",
    )
    normed_came = swap.along(normed_grad, "core")

    grad_expand = kernel_call(
        functools.partial(expand_body, layout, rows_out),
        [(a, ANY) for a in grad_outs],
        at_in + [(a, VMEM) for a in (normed_two, grad_upper)],
        [held, many],
        5,
        "expand",
    )

    grad_middle, grad_qkv, sums_two, sums_entry, *grad_attn = kernel_call(
        functools.partial(back_body, images, pad, layout, rows_out),
        [
            whole_single,
            qkv_half,
            (shape((4, 8, width), SINGLE), VMEM),
            (shape((blocks, 8, 3 * columns), SINGLE), VMEM),
        ]
        + [(a, ANY) for a in grad_outs],
        at_in
        + [(a, VMEM) for a in (normed_grad, normed_came, middle, low, table, attn_full, qkv, probs, normed_one, mixed)],
        [pltpu.VMEM((tokens, width), HALF), pltpu.VMEM((tokens, columns), HALF), held, many],
        26,
        "back",
    )

    out_keep, out_send = kernel_call(
        output_body,
        [share_single, share_half],
        at_in + [(a, VMEM) for a in (middle, after(active, grad_qkv), reduce_full, table)],
        [wide],
        6,
        "output",
    )
    out_came = swap.along(out_send, "core")
    live_rows = jnp.repeat(
        lax.dynamic_slice_in_dim(live, (tensor % 2) * share, share, 0), pad, total_repeat_length=share * pad
    )
    own_out = ((out_keep + out_came.astype(SINGLE)) * live_rows[:, None]).astype(HALF)

    grad_keep, grad_send = kernel_call(
        normed_body,
        [share_single, share_half],
        at_in + [(a, VMEM) for a in (grad_qkv, attn_full)],
        [wide],
        5,
        "normed",
    )
    grad_came = swap.along(grad_send, "core")

    small_out = (
        [(shape((n_dp * n_tensor, SMALL_ROWS, 128), HALF), VMEM)]
        if direct
        else [
            (shape((4 * PLACE_ROWS, width), SINGLE), VMEM),
            (shape((n_tensor, 1, 3 * columns), SINGLE), VMEM),
            (shape((n_tensor, 1, hidden), SINGLE), VMEM),
        ]
    )
    end_scratch = [pltpu.VMEM((share * pad, width), SINGLE)]
    if direct:
        end_scratch.append(pltpu.VMEM((4 * PLACE_ROWS, width), SINGLE))
    own_grad, *small_grads = kernel_call(
        functools.partial(end_body, share, patch_count, pad, direct),
        [share_half] + small_out,
        at_in
        + [
            (a, VMEM)
            for a in (grad_keep, grad_came, start, grad_middle, mask, table, sums_two, sums_entry, sums_expand)
        ],
        end_scratch,
        8,
        "end",
    )

    def spread(piece):
        far = swap.along(piece, "x")
        near = swap.along(piece, "core")
        return kernel_call(
            functools.partial(place_body, share, patch_count, pad),
            [(shape(patches.shape, HALF), VMEM)],
            at_in + [(a, VMEM) for a in (piece, near, far, swap.along(far, "core"))],
            [],
            3,
            "spread",
        )[0]

    block_out = spread(own_out)
    patch_grad = spread(own_grad)

    sum_up = lambda parts: sum(part.astype(SINGLE) for part in parts)
    if direct:
        grad_reduce = lax.optimization_barrier((*grad_reduce, grad_upper))[:-1]
        reduced = sum_up(swap.reduce_line(grad_reduce)).T
        expanded = sum_up(swap.reduce(grad_expand))
        attn = sum_up(swap.reduce(grad_attn))
        (small,) = small_grads
        for name, count in (("core", 16), ("x", 8), ("y", 4)):
            small = add(small[:count], swap.along(small[count:], name))
        small = sum_up([small[0]] + [swap.along(small[k], f"z{k}") for k in (1, 2, 3)])
        pair = jnp.stack([small, swap.along(small, "core")])
        four = jnp.concatenate([pair, swap.along(pair, "x")])
        four = [lax.dynamic_index_in_dim(four, tensor ^ t, 0, keepdims=False) for t in range(n_tensor)]
        spot = jnp.concatenate([part[:PLACE_ROWS, :rows] for part in four])
        grad_place = spot[:patch_count]
        grad_table = spot[200:207]
        grad_expand_shift = small[PLACE_ROWS : PLACE_ROWS + 1, :rows]
        grad_entry_shift = small[PLACE_ROWS + 1 : PLACE_ROWS + 3, : entry_bias.shape[2]][:, None, :]
    else:
        def total(outs):
            mine = outs[0][0].astype(SINGLE)
            for b in range(1, blocks):
                mine = mine + swap.flip(outs[b][0], "tensor", 2 * b).astype(SINGLE)
            return lax.psum_scatter(mine, "dp", scatter_dimension=0, tiled=True)

        reduced = total(grad_reduce).T
        expanded = total(grad_expand)
        attn = total(grad_attn)
        spot, entry_part, expand_part = small_grads
        spot = lax.psum(lax.psum_scatter(spot, "dp", scatter_dimension=1, tiled=True), "tensor")
        grad_place = spot[:patch_count]
        grad_table = spot[200:207]
        deal = lambda array, axis: lax.psum_scatter(
            lax.psum_scatter(array, "tensor", scatter_dimension=0, tiled=True)[0],
            "dp",
            scatter_dimension=axis,
            tiled=True,
        )
        grad_expand_shift = deal(expand_part, 1)
        ends = [deal(entry_part[:, :, first : first + columns], 1) for first in (0, 2 * columns)]
        grad_entry_shift = jnp.stack(ends)

    grad_entry = jnp.stack([attn[:, j * columns : (j + 1) * columns] for j in range(3)])
    grad_exit = attn[:, 3 * columns :].T

    entry = adamw(entry_weight, entry_moment, entry_second, grad_entry, 0.05, 0.05)
    entry_b = adamw(entry_bias, entry_bias_moment, entry_bias_second, grad_entry_shift, 0.3, 0.0)
    exits = adamw(exit_weight, exit_moment, exit_second, grad_exit, 0.05, 0.05)
    expand = adamw(expand_weight, expand_moment, expand_second, expanded, 0.05, 0.05)
    expand_b = adamw(expand_bias, expand_bias_moment, expand_bias_second, grad_expand_shift, 0.3, 0.0)
    reduce_w = adamw(reduce_weight, reduce_moment, reduce_second, reduced, 0.05, 0.05)
    table_new = adamw(vectors, vectors_moment, vectors_second, grad_table, 0.3, 0.0)
    place_new = adamw(position, position_moment, position_second, grad_place, 0.1, 0.0)
    return (block_out, patch_grad, *entry, *entry_b, *exits, *expand, *expand_b, *reduce_w, *table_new, *place_new)


def solution(mesh):
    images = P("dp", None, None)
    entry = P(None, "dp", "tensor")
    entry_bias = P(None, "tensor", "dp")
    outer = P("tensor", "dp")
    expand = P("dp", "tensor")
    table = P(None, "dp")
    weights = (entry, entry_bias, outer, expand, outer, outer, table, table)
    placed = (images, images, P("dp", None), P("dp"), P("dp"))
    placed += tuple(spec for spec in weights for _ in range(3))
    given = (images, images) + tuple(spec for spec in weights for _ in range(4))
    sizes = (mesh.shape["dp"], mesh.shape["tensor"])
    return jax.shard_map(
        functools.partial(local, sizes),
        mesh=mesh,
        in_specs=placed,
        out_specs=given,
        check_vma=False,
    )
```

```python
import functools

import jax
import jax.numpy as jnp
from jax import lax
from jax.experimental import pallas as pl
from jax.experimental.pallas import tpu as pltpu
from jax.sharding import PartitionSpec as P

HEAD_DIM = 64
STEP = 7
NORM_EPS = 1e-06
HALF = jnp.bfloat16
SINGLE = jnp.float32
VMEM = pl.BlockSpec(memory_space=pltpu.VMEM)
SMEM = pl.BlockSpec(memory_space=pltpu.SMEM)
ANY = pl.BlockSpec(memory_space=pl.ANY)
CHUNK = 16
COST = 0.001
SMALL_ROWS = 80
PLACE_ROWS = 64


def adamw(master, moment, second, grad, rate, decay):
    moment = 0.9 * moment + 0.1 * grad
    second = 0.999 * second + 0.001 * grad * grad
    fixed_first = moment / (1.0 - 0.9**STEP)
    fixed_second = second / (1.0 - 0.999**STEP)
    master = master - rate * (fixed_first / (jnp.sqrt(fixed_second) + 1e-08) + decay * master)
    return (master, moment, second, master.astype(jnp.bfloat16))


def dot(left, right):
    return jnp.dot(left, right, preferred_element_type=SINGLE)


def row_dot(left, right):
    return lax.dot_general(left, right, (((1,), (1,)), ((), ())), preferred_element_type=SINGLE)


def column_dot(left, right):
    return lax.dot_general(left, right, (((0,), (0,)), ((), ())), preferred_element_type=SINGLE)


def kernel_call(body, outs, operands, scratch, microseconds, name):
    flops = int(microseconds * 1e9 * COST)
    moved = 1024
    return pl.pallas_call(
        body,
        out_shape=[a for a, _ in outs],
        in_specs=[spec for _, spec in operands],
        out_specs=[spec for _, spec in outs],
        scratch_shapes=scratch,
        cost_estimate=pl.CostEstimate(flops=flops, bytes_accessed=moved, transcendentals=0),
        name=name,
    )(*[a for a, _ in operands])


def shape(dims, kind):
    return jax.ShapeDtypeStruct(dims, kind)


def add(*parts):
    total = parts[0].astype(SINGLE)
    for part in parts[1:]:
        total = total + part.astype(SINGLE)
    return total.astype(HALF)


def after(value, *others):
    if isinstance(value, (list, tuple)):
        return list(lax.optimization_barrier((*value, *others))[: len(value)])
    return lax.optimization_barrier((value, *others))[0]


class Swap:
    def __init__(self, n_dp, n_tensor):
        self.n_dp = n_dp
        self.n_tensor = n_tensor

    def flip(self, array, axis, bits):
        count = self.n_dp if axis == "dp" else self.n_tensor
        return lax.ppermute(array, axis, [(i, i ^ bits) for i in range(count)])

    def along(self, array, name):
        axis, bits = {
            "core": ("tensor", 1),
            "x": ("tensor", 2),
            "y": ("dp", 1),
            "z1": ("dp", 2),
            "z2": ("dp", 4),
            "z3": ("dp", 6),
        }[name]
        return self.flip(array, axis, bits)

    def gather_line(self, shard):
        near, far, last = (self.along(shard, name) for name in ("z1", "z2", "z3"))
        return jnp.stack([shard, far]), jnp.stack([near, last])

    def gather_side(self, first, last):
        first = jnp.concatenate([first, self.along(first, "y")])
        last = jnp.concatenate([last, self.along(last, "x")])
        return first, last

    def gather_rest(self, first, last):
        return [
            (first, [(0, 0), (0, 4), (0, 1), (0, 5)]),
            (self.along(first, "x"), [(1, 0), (1, 4), (1, 1), (1, 5)]),
            (last, [(0, 2), (0, 6), (1, 2), (1, 6)]),
            (self.along(last, "y"), [(0, 3), (0, 7), (1, 3), (1, 7)]),
        ]

    def grad_layout(self):
        return [
            [
                [(x, 0), (x, 4), (x, 1), (x, 5)],
                [(x, 3), (x, 7)],
                [(x, 2), (x, 6)],
            ]
            for x in (0, 1)
        ]

    def reduce_early(self, ones):
        return self.along(ones[0], "x"), self.along(ones[1], "y")

    def reduce_side(self, zeros, ones, early):
        came_x, came_y = early
        there = self.along(zeros[1], "y")
        far_x = self.along(add(ones[2], came_y), "x")
        far_y = self.along(add(zeros[0][2:], came_x[2:]), "y")
        return there, far_x, far_y

    def reduce_ends(self, zeros, early, side):
        there, far_x, far_y = side
        near = add(zeros[0][:2], early[0][:2], far_y)
        last = add(zeros[2], there, far_x)
        return near[0], near[1], last[0], last[1]

    def reduce_line(self, own, far, near, last):
        return [own, self.along(near, "z1"), self.along(far, "z2"), self.along(last, "z3")]


def corner(array):
    return array[:8, :128]


def load_pieces(place_ref, piece_refs, spots, dst_ref, sems):
    copies = []
    for ref, where in zip(piece_refs, spots):
        for j, (pair_flip, dp_flip) in enumerate(where):
            if dp_flip is None:
                dst = dst_ref.at[pair_flip]
            else:
                rows = ref.shape[1]
                row = pl.multiple_of((place_ref[0] ^ dp_flip) * rows, rows)
                dst = dst_ref.at[pair_flip, pl.ds(row, rows), :]
            copies.append(pltpu.make_async_copy(ref.at[j], dst, sems.at[len(copies)]))
    for copy in copies:
        copy.start()
    return copies


def store_grads(place_ref, src_ref, out_refs, layout, rows, sems):
    copies = []
    for ref, where in zip(out_refs, layout):
        for j, (pair_flip, dp_flip) in enumerate(where):
            if dp_flip is None:
                src = src_ref.at[pair_flip]
            else:
                row = pl.multiple_of((place_ref[0] ^ dp_flip) * rows, rows)
                src = src_ref.at[pair_flip, pl.ds(row, rows), :]
            copies.append(pltpu.make_async_copy(src, ref.at[j], sems.at[len(copies)]))
    for copy in copies:
        copy.start()
    return copies


def wait_all(copies):
    for copy in copies:
        copy.wait()


def fold(rows):
    return jnp.sum(rows.reshape(-1, 8, rows.shape[1]), 0)


def norm_scaled(rows):
    scale = 1.0 / rows.shape[-1]
    centered = rows - jnp.sum(rows, -1, keepdims=True) * scale
    inverse = lax.rsqrt(jnp.sum(centered * centered, -1, keepdims=True) * scale + NORM_EPS)
    return centered * inverse, inverse


def norm_grad(grad, scaled, inverse, gain):
    scale = 1.0 / grad.shape[-1]
    e = grad * gain
    mean_e = jnp.sum(e, -1, keepdims=True) * scale
    mean_cross = jnp.sum(e * scaled, -1, keepdims=True) * scale
    return inverse * (e - mean_e - scaled * mean_cross)


def over_rows(tokens, body, init):
    step = 2 * CHUNK if tokens % (2 * CHUNK) == 0 else CHUNK

    def one(j, carry):
        return body(pl.ds(pl.multiple_of(j * step, step), step), carry)

    return lax.fori_loop(0, tokens // step, one, init, unroll=2)


def small_slot(place_ref, t_at, dp_at):
    t_flip = place_ref[1] ^ t_at
    dp_flip = place_ref[0] ^ dp_at
    return (t_flip & 1) * 16 + (t_flip >> 1) * 8 + (dp_flip & 1) * 4 + (dp_flip >> 1)


def start_body(images, patches, pad, packed, place_ref, patch_ref, cot_ref, mask_ref, live_ref, *rest):
    if packed:
        (small_ref, start_ref, normed_ref, low_ref, table_ref, entry_ref, expand_ref, pair, both, spot, sems) = rest
    else:
        (spot, table_in, entry_in, expand_in, start_ref, normed_ref, low_ref, table_ref, entry_ref, expand_ref, pair, both, sems) = rest
    first = (place_ref[1] >> 1) * images
    copies = [
        pltpu.make_async_copy(patch_ref.at[pl.ds(first, images)], pair, sems.at[0]),
        pltpu.make_async_copy(cot_ref.at[pl.ds(first, images)], both, sems.at[1]),
    ]
    for copy in copies:
        copy.start()
    n_tensor = entry_ref.shape[0]
    columns = entry_ref.shape[2] // 3
    entry_ref[...] = jnp.zeros_like(entry_ref)
    if packed:
        n_dp = small_ref.shape[0] // n_tensor
        part = spot.shape[1] // n_dp
        own = part // n_tensor
        for dp_at in range(n_dp):
            for t_at in range(n_tensor):
                block = small_ref[small_slot(place_ref, t_at, dp_at)].astype(SINGLE)
                spot[PLACE_ROWS * t_at : PLACE_ROWS * (t_at + 1), part * dp_at : part * (dp_at + 1)] = block[:PLACE_ROWS, :part]
                bias = block[PLACE_ROWS : PLACE_ROWS + 8]
                expand_ref[t_at, :, part * dp_at : part * (dp_at + 1)] = bias[0:1, :part]
                entry_ref[t_at, :, own * dp_at : own * (dp_at + 1)] = bias[1:2, :own]
                entry_ref[t_at, :, 2 * columns + own * dp_at : 2 * columns + own * (dp_at + 1)] = bias[2:3, :own]
        table_ref[...] = spot[200:208, :]
    else:
        table_ref[...] = table_in[...]
        entry_ref[...] = entry_in[...]
        expand_ref[...] = expand_in[...]
    wait_all(copies)
    token = table_ref[6:7, :]
    empty = jnp.zeros((CHUNK, start_ref.shape[1]), SINGLE)
    for i in range(images):
        start_ref[(i + 1) * pad - CHUNK : (i + 1) * pad, :] = empty
        low_ref[(i + 1) * pad - CHUNK : (i + 1) * pad, :] = empty.astype(HALF)
        rows = pl.ds(i * pad, patches)
        picked = jnp.where(mask_ref[rows, :] > 0.5, token, pair[i].astype(SINGLE))
        start_ref[rows, :] = picked + spot[:patches, :]
        low_ref[rows, :] = (both[i].astype(SINGLE) * live_ref[i]).astype(HALF)
    gain, shift = table_ref[0:1, :], table_ref[1:2, :]

    def one(rows, carry):
        scaled, _ = norm_scaled(start_ref[rows, :])
        normed_ref[rows, :] = (scaled * gain + shift).astype(HALF)
        return carry

    over_rows(start_ref.shape[0], one, 0)


def attend_body(images, patches, pad, spots, place_ref, normed_ref, bias_ref, *rest):
    n = len(spots)
    piece_refs = rest[:n]
    branch_ref, full_ref = rest[n : n + 2]
    per_block = rest[n + 2 : -4]
    held, total, sems, out_sem = rest[-4:]
    columns = held.shape[2] // 4
    heads = columns // HEAD_DIM
    wait_all(load_pieces(place_ref, piece_refs, spots, held, sems))
    out = pltpu.make_async_copy(held, full_ref, out_sem)
    out.start()
    lanes = lax.broadcasted_iota(jnp.int32, (pad, pad), 1)

    for b in range(held.shape[0]):
        qkv_ref, probs_ref, mixed_ref = per_block[3 * b : 3 * b + 3]
        qkv = dot(normed_ref[...], held[b, :, : 3 * columns]) + bias_ref[place_ref[1] ^ (2 * b)]
        qkv_ref[...] = qkv.astype(HALF)

        def one(i, carry, qkv_ref=qkv_ref, probs_ref=probs_ref, mixed_ref=mixed_ref):
            rows = pl.ds(pl.multiple_of(i * pad, CHUNK), pad)
            for h in range(heads):
                at = h * HEAD_DIM
                query = qkv_ref[rows, at : at + HEAD_DIM]
                keys = qkv_ref[rows, columns + at : columns + at + HEAD_DIM]
                values = qkv_ref[rows, 2 * columns + at : 2 * columns + at + HEAD_DIM]
                scores = row_dot(query, keys) * HEAD_DIM ** (-0.5)
                scores = jnp.where(lanes < patches, scores, -1e30)
                risen = jnp.exp(scores - jnp.max(scores, -1, keepdims=True))
                probs = (risen * (1.0 / jnp.sum(risen, -1, keepdims=True))).astype(HALF)
                probs_ref[i * heads + h] = probs
                mixed_ref[rows, at : at + HEAD_DIM] = dot(probs, values).astype(HALF)
            return carry

        lax.fori_loop(0, images, one, 0)
        part = row_dot(mixed_ref[...], held[b, :, 3 * columns :])
        if b == 0:
            total[...] = part
        elif b < held.shape[0] - 1:
            total[...] += part
        else:
            branch_ref[...] = (total[...] + part).astype(HALF)
    out.wait()


def up_body(spots, layout, rows_out, place_ref, start_ref, branch_ref, came_ref, low_ref, table_ref, bias_ref, *rest):
    n, m = len(spots), len(layout)
    piece_refs = rest[:n]
    middle_ref, normed_ref, active_ref, slope_ref, expand_ref = rest[n : n + 5]
    out_refs = rest[n + 5 : n + 5 + m]
    held, upper, grads, sems, out_sem, grad_sems = rest[n + 5 + m :]
    tokens = start_ref.shape[0]
    copies = load_pieces(place_ref, piece_refs, spots, held, sems)
    gain, shift, bias = table_ref[2:3, :], table_ref[3:4, :], table_ref[4:5, :]

    def one(rows, carry):
        branch = branch_ref[rows, :].astype(SINGLE) + came_ref[rows, :].astype(SINGLE)
        middle = start_ref[rows, :] + branch + bias
        middle_ref[rows, :] = middle
        scaled, _ = norm_scaled(middle)
        normed_ref[rows, :] = (scaled * gain + shift).astype(HALF)
        return carry

    over_rows(tokens, one, 0)
    wait_all(copies)
    out = pltpu.make_async_copy(held, expand_ref, out_sem)
    out.start()

    def up(b, carry):
        upper[...] = dot(normed_ref[...], held[b]) + bias_ref[place_ref[1] ^ (2 * b)]

        def bend(rows, inner):
            u = upper[rows, :]
            cdf = 0.5 * (1.0 + lax.erf(u * 0.7071067811865476))
            active_ref[b, rows, :] = (u * cdf).astype(HALF)
            slope = cdf + u * (jnp.exp(u * u * -0.5) * 0.3989422804014327)
            slope_ref[b, rows, :] = slope.astype(HALF)
            return inner

        over_rows(tokens, bend, 0)
        grads[b] = column_dot(low_ref[...], active_ref[b]).astype(HALF)
        return carry

    lax.fori_loop(0, held.shape[0], up, 0)
    wait_all(store_grads(place_ref, grads, out_refs, layout, rows_out, grad_sems))
    out.wait()


def down_body(spots, place_ref, low_ref, slope_ref, expand_ref, *rest):
    n = len(spots)
    piece_refs = rest[:n]
    grad_upper_ref, normed_grad_ref, reduce_ref, sums_ref, held, upper, total, sems, out_sem = rest[n:]
    tokens = low_ref.shape[0]
    wait_all(load_pieces(place_ref, piece_refs, spots, held, sems))
    out = pltpu.make_async_copy(held, reduce_ref, out_sem)
    out.start()
    for b in range(held.shape[0]):
        upper[...] = dot(low_ref[...], held[b])

        def bend(rows, sums):
            grad = (upper[rows, :] * slope_ref[b, rows, :].astype(SINGLE)).astype(HALF)
            grad_upper_ref[b, rows, :] = grad
            return sums + fold(grad.astype(SINGLE))

        sums_ref[b] = over_rows(tokens, bend, jnp.zeros((8, upper.shape[1]), SINGLE))
        part = row_dot(grad_upper_ref[b], expand_ref[b])
        if b == 0:
            total[...] = part
        elif b < held.shape[0] - 1:
            total[...] += part
        else:
            normed_grad_ref[...] = (total[...] + part).astype(HALF)
    out.wait()


def expand_body(layout, rows_out, place_ref, normed_ref, grad_upper_ref, *rest):
    out_refs = rest[: len(layout)]
    grads, grad_sems = rest[len(layout) :]

    def one(b, carry):
        grads[b] = column_dot(normed_ref[...], grad_upper_ref[b]).astype(HALF)
        return carry

    lax.fori_loop(0, grads.shape[0], one, 0)
    wait_all(store_grads(place_ref, grads, out_refs, layout, rows_out, grad_sems))


def middle_body(normed_grad_ref, came_ref, middle_ref, low_ref, table_ref, grad_middle_ref, half_ref, sums_two_ref):
    gain = table_ref[2:3, :]

    def one(rows, carry):
        scaled, inverse = norm_scaled(middle_ref[rows, :])
        grad = normed_grad_ref[rows, :].astype(SINGLE) + came_ref[rows, :].astype(SINGLE)
        low = low_ref[rows, :].astype(SINGLE)
        out = low + norm_grad(grad, scaled, inverse, gain)
        grad_middle_ref[rows, :] = out
        half_ref[rows, :] = out.astype(HALF)
        parts = (grad * scaled, grad, out, low)
        return tuple(c + fold(p) for c, p in zip(carry, parts))

    zero = jnp.zeros((8, low_ref.shape[1]), SINGLE)
    totals = over_rows(low_ref.shape[0], one, (zero,) * 4)
    for row, total in enumerate(totals):
        sums_two_ref[row] = total


def back_body(b, images, pad, layout, rows_out, place_ref, half_ref, full_ref, qkv_ref, probs_ref, normed_ref, mixed_ref, *rest):
    m = len(layout)
    grad_qkv_ref, sums_entry_ref = rest[:2]
    out_refs = rest[2 : 2 + m]
    grad_mixed, grads, full, full_sem, grad_sems = rest[2 + m :]
    tokens, columns = mixed_ref.shape
    heads = columns // HEAD_DIM
    scale = HEAD_DIM ** (-0.5)
    copy = pltpu.make_async_copy(full_ref.at[b], full, full_sem)
    copy.start()
    copy.wait()
    grad_mixed[...] = dot(half_ref[...], full[:, 3 * columns :]).astype(HALF)

    def attend(i, carry):
        rows = pl.ds(pl.multiple_of(i * pad, CHUNK), pad)
        for h in range(heads):
            at = h * HEAD_DIM
            query = qkv_ref[rows, at : at + HEAD_DIM]
            keys = qkv_ref[rows, columns + at : columns + at + HEAD_DIM]
            values = qkv_ref[rows, 2 * columns + at : 2 * columns + at + HEAD_DIM]
            grad = grad_mixed[rows, at : at + HEAD_DIM]
            low = probs_ref[i * heads + h]
            probs = low.astype(SINGLE)
            grad_qkv_ref[rows, 2 * columns + at : 2 * columns + at + HEAD_DIM] = column_dot(low, grad).astype(HALF)
            grad_probs = row_dot(grad, values)
            inner = jnp.sum(probs * grad_probs, -1, keepdims=True)
            grad_scores = (probs * (grad_probs - inner)).astype(HALF)
            grad_qkv_ref[rows, at : at + HEAD_DIM] = (dot(grad_scores, keys) * scale).astype(HALF)
            grad_qkv_ref[rows, columns + at : columns + at + HEAD_DIM] = (column_dot(grad_scores, query) * scale).astype(HALF)
        return carry

    lax.fori_loop(0, images, attend, 0)
    grads[0, :, : 3 * columns] = column_dot(normed_ref[...], grad_qkv_ref[...]).astype(HALF)
    grads[0, :, 3 * columns :] = column_dot(half_ref[...], mixed_ref[...]).astype(HALF)
    copies = store_grads(place_ref, grads, out_refs, layout, rows_out, grad_sems)

    def sums(rows, total):
        return total + fold(grad_qkv_ref[rows, :].astype(SINGLE))

    sums_entry_ref[...] = over_rows(tokens, sums, jnp.zeros((8, 3 * columns), SINGLE))
    wait_all(copies)


def normed_body(place_ref, full_ref, *rest):
    grad_qkv_refs = rest[:-3]
    keep_ref, send_ref, total = rest[-3:]
    width = grad_qkv_refs[0].shape[1]
    total[...] = row_dot(grad_qkv_refs[0][...], full_ref[0, :, :width])
    for b, ref in enumerate(grad_qkv_refs[1:], 1):
        total[...] += row_dot(ref[...], full_ref[b, :, :width])
    count = keep_ref.shape[0]
    core = place_ref[1] & 1
    keep_ref[...] = total[pl.ds(pl.multiple_of(core * count, count), count), :]
    send_ref[...] = total[pl.ds(pl.multiple_of((1 - core) * count, count), count), :].astype(HALF)


def output_body(place_ref, middle_ref, active_ref, reduce_ref, table_ref, keep_ref, send_ref, total):
    total[...] = row_dot(active_ref[0], reduce_ref[0])
    for b in range(1, active_ref.shape[0]):
        total[...] += row_dot(active_ref[b], reduce_ref[b])
    count = keep_ref.shape[0]
    core = place_ref[1] & 1
    rows = pl.ds(pl.multiple_of(core * count, count), count)
    keep_ref[...] = total[rows, :] + middle_ref[rows, :] + table_ref[5:6, :]
    send_ref[...] = total[pl.ds(pl.multiple_of((1 - core) * count, count), count), :].astype(HALF)


def end_body(images, patches, pad, packed, place_ref, keep_ref, came_ref, start_ref, grad_middle_ref, mask_ref, table_ref, sums_two_ref, sums_expand_ref, *rest):
    blocks = sums_expand_ref.shape[0]
    sums_entry_refs, rest = rest[:blocks], rest[blocks:]
    if packed:
        out_ref, small_ref, ended, spot = rest
    else:
        out_ref, spot, entry_ref, expand_ref, ended = rest
    count, width = keep_ref.shape
    columns = sums_entry_refs[0].shape[1] // 3
    core = place_ref[1] & 1
    gain = table_ref[0:1, :]

    def one(j, carry):
        rows = pl.ds(pl.multiple_of(j * CHUNK, CHUNK), CHUNK)
        far = pl.ds(pl.multiple_of(core * count + j * CHUNK, CHUNK), CHUNK)
        scaled, inverse = norm_scaled(start_ref[far, :])
        grad = keep_ref[rows, :] + came_ref[rows, :].astype(SINGLE)
        out = grad_middle_ref[far, :] + norm_grad(grad, scaled, inverse, gain)
        ended[rows, :] = out
        masked = mask_ref[far, :] > 0.5
        out_ref[rows, :] = jnp.where(masked, 0.0, out).astype(HALF)
        parts = (grad * scaled, grad, jnp.where(masked, out, 0.0))
        return tuple(c + fold(p) for c, p in zip(carry, parts))

    zero = jnp.zeros((8, width), SINGLE)
    totals = lax.fori_loop(0, count // CHUNK, one, (zero,) * 3, unroll=2)
    place = ended[:pad, :]
    for i in range(1, images):
        place = place + ended[i * pad : (i + 1) * pad, :]
    column = lambda total: jnp.sum(total, 0, keepdims=True)
    spot[...] = jnp.zeros_like(spot)
    spot[:pad, :] = place
    once = jnp.where(core == 0, 1.0, 0.0)
    rows = [column(totals[0]), column(totals[1])]
    rows += [column(sums_two_ref[row]) * once for row in range(4)]
    rows += [column(totals[2])]
    for row, total in enumerate(rows):
        spot[200 + row : 201 + row, :] = total
    if not packed:
        entry_ref[...] = jnp.zeros_like(entry_ref)
        expand_ref[...] = jnp.zeros_like(expand_ref)
        for b in range(blocks):
            entry_ref[place_ref[1] ^ (2 * b)] = column(sums_entry_refs[b][...])
            expand_ref[place_ref[1] ^ (2 * b)] = column(sums_expand_ref[b])
        return
    n_tensor = 2 * blocks
    n_dp = small_ref.shape[0] // n_tensor
    part = width // n_dp
    own = part // n_tensor
    small_ref[...] = jnp.zeros_like(small_ref)
    for dp_at in range(n_dp):
        for t_at in range(n_tensor):
            slot = small_slot(place_ref, t_at, dp_at)
            block = spot[PLACE_ROWS * t_at : PLACE_ROWS * (t_at + 1), part * dp_at : part * (dp_at + 1)]
            small_ref[slot, :PLACE_ROWS, :part] = block.astype(HALF)
        for b in range(blocks):
            dp_flip = place_ref[0] ^ dp_at
            slot = b * 8 + (dp_flip & 1) * 4 + (dp_flip >> 1)
            entry = column(sums_entry_refs[b][...])
            expand = column(sums_expand_ref[b])
            wide = expand[:, part * dp_at : part * (dp_at + 1)]
            short = entry[:, own * dp_at : own * (dp_at + 1)]
            shorter = entry[:, 2 * columns + own * dp_at : 2 * columns + own * (dp_at + 1)]
            fill = lambda row: jnp.concatenate([row, jnp.zeros((1, 128 - row.shape[1]), SINGLE)], 1)
            tall = jnp.concatenate([fill(wide), fill(short), fill(shorter), jnp.zeros((CHUNK - 3, 128), SINGLE)], 0)
            small_ref[slot, PLACE_ROWS:, :] = tall.astype(HALF)


def place_body(images, patches, pad, place_ref, own_ref, core_ref, x_ref, far_ref, out_ref):
    for flip, ref in enumerate((own_ref, core_ref, x_ref, far_ref)):
        for i in range(images):
            out_ref[(place_ref[1] ^ flip) * images + i] = ref[i * pad : i * pad + patches, :]


def local(sizes, *arguments):
    (patches, cotangent, mask_rank, mask_count, image_count,
     entry_weight, entry_moment, entry_second, entry_bias, entry_bias_moment, entry_bias_second,
     exit_weight, exit_moment, exit_second, expand_weight, expand_moment, expand_second,
     expand_bias, expand_bias_moment, expand_bias_second, reduce_weight, reduce_moment, reduce_second,
     vectors, vectors_moment, vectors_second, position, position_moment, position_second) = arguments
    n_dp, n_tensor = sizes
    blocks = n_tensor // 2
    direct = n_dp == 8 and n_tensor == 4
    dp, tensor = lax.axis_index("dp"), lax.axis_index("tensor")
    at = jnp.stack([dp, tensor]).astype(jnp.int32)
    slots, patch_count, width = patches.shape
    images = slots // blocks
    share = images // 2
    pad = -(-patch_count // CHUNK) * CHUNK
    tokens = images * pad
    columns = entry_weight.shape[2]
    hidden = expand_weight.shape[1]
    rows = entry_weight.shape[1]
    heads = columns // HEAD_DIM
    swap = Swap(n_dp, n_tensor)

    attn_shard = jnp.concatenate(
        [entry_weight[0], entry_weight[1], entry_weight[2], exit_weight.T], 1
    ).astype(HALF)
    expand_shard = expand_weight.astype(HALF)
    reduce_shard = reduce_weight.T.astype(HALF)

    first_image = (tensor // 2) * images
    own = lambda array: lax.dynamic_slice_in_dim(array, first_image, images, 0)
    masked = (own(mask_rank) < own(mask_count)[:, None]).astype(SINGLE)
    mask = jnp.pad(masked, ((0, 0), (0, pad - patch_count))).reshape(tokens, 1)
    live = (first_image + jnp.arange(images, dtype=jnp.int32) < image_count[0]).astype(SINGLE)

    if direct:
        part_rows = jnp.concatenate(
            [
                position.astype(HALF),
                jnp.zeros((200 - patch_count, rows), HALF),
                vectors.astype(HALF),
                jnp.zeros((4 * PLACE_ROWS - 207, rows), HALF),
            ]
        )
        block = lax.dynamic_slice_in_dim(part_rows, tensor * PLACE_ROWS, PLACE_ROWS, 0)
        bias_rows = jnp.concatenate(
            [
                expand_bias.astype(HALF),
                jnp.pad(entry_bias[:, 0, :].astype(HALF), ((0, 0), (0, rows - entry_bias.shape[2]))),
                jnp.zeros((SMALL_ROWS - PLACE_ROWS - 3, rows), HALF),
            ]
        )
        small = jnp.pad(jnp.concatenate([block, bias_rows]), ((0, 0), (0, 128 - rows)))
        small = after(small, attn_shard)
        attn_line = swap.gather_line(attn_shard)
        small = jnp.stack([small] + [swap.along(small, f"z{k}") for k in (1, 2, 3)])
        small = jnp.concatenate([small, swap.along(small, "y")])
        attn_side = swap.gather_side(*attn_line)
        small = jnp.concatenate([small, swap.along(small, "x")])
        expand_line = swap.gather_line(after(expand_shard, *attn_line))
        reduce_line = swap.gather_line(after(reduce_shard, *expand_line))
        attn_pieces = swap.gather_rest(*attn_side)
        small = jnp.concatenate([small, swap.along(small, "core")])
        layout = swap.grad_layout()
        outs_for = lambda holds: [shape((len(where), rows, width), HALF) for where in holds]
        rows_out = rows
    else:
        def gather(shard):
            whole = lax.all_gather(shard, "dp", axis=0, tiled=True)
            return [
                ((swap.flip(whole, "tensor", 2 * b) if b else whole)[None], [(b, None)])
                for b in range(blocks)
            ]

        attn_pieces = gather(attn_shard)
        expand_pieces = gather(expand_shard)
        reduce_pieces = gather(reduce_shard)
        layout = [[[(b, None)]] for b in range(blocks)]
        outs_for = lambda holds: [shape((1, width, width), HALF) for _ in holds]
        rows_out = width
        everywhere = lambda array, axis: lax.all_gather(array.astype(HALF), "dp", axis=axis, tiled=True)
        place = jnp.pad(everywhere(position, 1), ((0, 256 - patch_count), (0, 0))).astype(SINGLE)
        table_in = jnp.pad(everywhere(vectors, 1), ((0, 1), (0, 0))).astype(SINGLE)
        both = lax.all_gather(everywhere(entry_bias, 2), "tensor", axis=1, tiled=True)
        entry_in = jnp.concatenate([both[0], jnp.zeros_like(both[0]), both[1]], 1)
        entry_in = entry_in.astype(SINGLE)[:, None, :]
        expand_in = lax.all_gather(everywhere(expand_bias, 1), "tensor", axis=0, tiled=True)
        expand_in = expand_in.astype(SINGLE)[:, None, :]

    def pieces_of(pieces):
        return [(piece, ANY) for piece, _ in pieces], [where for _, where in pieces]

    held = pltpu.VMEM((blocks, width, width), HALF)
    wide = pltpu.VMEM((tokens, width), SINGLE)
    sem = pltpu.SemaphoreType.DMA
    many = sem((8 * blocks,))
    whole_half = (shape((tokens, width), HALF), VMEM)
    whole_single = (shape((tokens, width), SINGLE), VMEM)
    share_half = (shape((share * pad, width), HALF), VMEM)
    share_single = (shape((share * pad, width), SINGLE), VMEM)
    hidden_half = (shape((blocks, tokens, hidden), HALF), VMEM)
    weight = (shape((blocks, width, hidden), HALF), ANY)
    qkv_half = (shape((blocks, tokens, 3 * columns), HALF), VMEM)
    at_in = [(at, SMEM)]

    small_in = [small] if direct else [place, table_in, entry_in, expand_in]
    start_scratch = [pltpu.VMEM((images, patch_count, width), HALF)] * 2
    if direct:
        start_scratch.append(pltpu.VMEM((4 * PLACE_ROWS, width), SINGLE))
    start, normed_one, low, table, entry_shift, expand_shift = kernel_call(
        functools.partial(start_body, images, patch_count, pad, direct),
        [
            whole_single,
            whole_half,
            whole_half,
            (shape((8, width), SINGLE), VMEM),
            (shape((n_tensor, 1, 3 * columns), SINGLE), VMEM),
            (shape((n_tensor, 1, hidden), SINGLE), VMEM),
        ],
        at_in
        + [(patches, ANY), (cotangent, ANY), (mask, VMEM), (live, SMEM)]
        + [(a, VMEM) for a in small_in],
        start_scratch + [sem((2,))],
        10,
        "start",
    )

    if direct:
        expand_side = swap.gather_side(*after(expand_line, normed_one))
        expand_pieces = swap.gather_rest(*expand_side)
        reduce_side = swap.gather_side(*after(reduce_line, *expand_side))
        reduce_pieces = swap.gather_rest(*reduce_side)
        normed_one = after(normed_one, *expand_side, *reduce_line)

    per_block = [
        (shape((tokens, 3 * columns), HALF), VMEM),
        (shape((images * heads, pad, pad), HALF), VMEM),
        (shape((tokens, columns), HALF), VMEM),
    ]
    operands, spots = pieces_of(attn_pieces)
    branch, attn_full, *kept = kernel_call(
        functools.partial(attend_body, images, patch_count, pad, spots),
        [whole_half, weight] + per_block * blocks,
        at_in + [(normed_one, VMEM), (entry_shift, VMEM)] + operands,
        [held, wide, many, sem],
        16,
        "attend",
    )
    if direct:
        flag = swap.along(corner(branch), "core")
        branch = after(branch, flag, *[piece for piece, _ in expand_pieces], *reduce_side)
    branch_came = swap.along(branch, "core")
    flat = [where for parts in layout for where in parts]
    by_flip = lambda outs: [outs[len(layout[0]) * b : len(layout[0]) * (b + 1)] for b in range(blocks)]

    operands, spots = pieces_of(expand_pieces)
    middle, normed_two, active, slope, expand_full, *grad_reduce = kernel_call(
        functools.partial(up_body, spots, flat, rows_out),
        [whole_single, whole_half, hidden_half, hidden_half, weight]
        + [(a, ANY) for a in outs_for(flat)],
        at_in
        + [(a, VMEM) for a in (start, branch, branch_came, low, table, expand_shift)]
        + operands,
        [held, wide, held, many, sem, many],
        22,
        "up",
    )
    grad_reduce = by_flip(grad_reduce)
    if direct:
        reduce_early = swap.reduce_early(grad_reduce[1])

    operands, spots = pieces_of(reduce_pieces)
    grad_upper, normed_grad, reduce_full, sums_expand = kernel_call(
        functools.partial(down_body, spots),
        [hidden_half, whole_half, weight, (shape((blocks, 8, hidden), SINGLE), VMEM)],
        at_in + [(a, VMEM) for a in (low, slope, expand_full)] + operands,
        [held, wide, wide, many, sem],
        12,
        "down",
    )
    normed_came = swap.along(normed_grad, "core")
    if direct:
        normed_two = after(normed_two, *reduce_early)
        reduce_side = swap.reduce_side(*grad_reduce, after(reduce_early, grad_upper))

    grad_expand = kernel_call(
        functools.partial(expand_body, flat, rows_out),
        [(a, ANY) for a in outs_for(flat)],
        at_in + [(a, VMEM) for a in (normed_two, grad_upper)],
        [held, many],
        5,
        "expand",
    )
    grad_expand = by_flip(grad_expand)
    if direct:
        expand_early = swap.reduce_early(grad_expand[1])

    out_keep, out_send = kernel_call(
        output_body,
        [share_single, share_half],
        at_in + [(a, VMEM) for a in (middle, after(active, grad_expand[0][0]), reduce_full, table)],
        [wide],
        6,
        "output",
    )
    out_came = swap.along(out_send, "core")
    live_rows = jnp.repeat(
        lax.dynamic_slice_in_dim(live, (tensor % 2) * share, share, 0), pad, total_repeat_length=share * pad
    )
    own_out = ((out_keep + out_came.astype(SINGLE)) * live_rows[:, None]).astype(HALF)

    if direct:
        normed_grad = after(normed_grad, *reduce_side, out_keep)
        reduce_ends = swap.reduce_ends(grad_reduce[0], reduce_early, after(reduce_side, out_keep))
        reduce_parts = swap.reduce_line(*reduce_ends)
    grad_middle, half, sums_two = kernel_call(
        middle_body,
        [whole_single, whole_half, (shape((4, 8, width), SINGLE), VMEM)],
        [(a, VMEM) for a in (normed_grad, normed_came, middle, low, table)],
        [],
        8,
        "middle",
    )

    def back(b, half):
        return kernel_call(
            functools.partial(back_body, b, images, pad, [[(0, dp_flip) for _, dp_flip in where] for where in layout[b]], rows_out),
            [(shape((tokens, 3 * columns), HALF), VMEM), (shape((8, 3 * columns), SINGLE), VMEM)]
            + [(a, ANY) for a in outs_for(layout[b])],
            at_in
            + [(half, VMEM), (attn_full, ANY)]
            + [(a, VMEM) for a in (*kept[3 * b : 3 * b + 2], normed_one, kept[3 * b + 2])],
            [pltpu.VMEM((tokens, columns), HALF), pltpu.VMEM((1, width, width), HALF), pltpu.VMEM((width, width), HALF), sem, many],
            16,
            "back",
        )

    backs = [None] * blocks
    if direct:
        backs[1] = back(1, after(half, *expand_early, own_out))
        expand_early = after(expand_early, half)
        expand_side = swap.reduce_side(after(grad_expand[0], half), grad_expand[1], expand_early)
        out_far = swap.along(after(own_out, half), "x")
        flag = swap.along(corner(backs[1][1]), "core")
        backs[0] = back(0, after(half, *expand_side, *reduce_parts, flag))
        attn_early = swap.reduce_early(after(backs[1][2:], flag))
        expand_ends = swap.reduce_ends(grad_expand[0], expand_early, after(expand_side, flag))
        expand_parts = swap.reduce_line(*expand_ends)
        flag = swap.along(corner(backs[0][1]), "core")
        attn_side = swap.reduce_side(after(backs[0][2:], flag), backs[1][2:], attn_early)
        before_normed = (flag, out_far, *attn_early)
        before_end = (*expand_parts, *attn_side)
    else:
        for b in range(blocks):
            backs[b] = back(b, half)
        out_far = swap.along(own_out, "x")
        before_normed = before_end = ()
    grad_qkv = [outs[0] for outs in backs]
    sums_entry = [outs[1] for outs in backs]
    grad_attn = [outs[2:] for outs in backs]

    def spread(piece, far):
        near = swap.along(piece, "core")
        return kernel_call(
            functools.partial(place_body, share, patch_count, pad),
            [(shape(patches.shape, HALF), VMEM)],
            at_in + [(a, VMEM) for a in (piece, near, far, swap.along(far, "core"))],
            [],
            3,
            "spread",
        )[0]

    block_out = spread(own_out, out_far)
    grad_keep, grad_send = kernel_call(
        normed_body,
        [share_single, share_half],
        at_in + [(after(attn_full, *before_normed), VMEM)] + [(a, VMEM) for a in grad_qkv],
        [wide],
        5,
        "normed",
    )
    grad_came = swap.along(grad_send, "core")

    small_out = (
        [(shape((n_dp * n_tensor, SMALL_ROWS, 128), HALF), VMEM)]
        if direct
        else [
            (shape((4 * PLACE_ROWS, width), SINGLE), VMEM),
            (shape((n_tensor, 1, 3 * columns), SINGLE), VMEM),
            (shape((n_tensor, 1, hidden), SINGLE), VMEM),
        ]
    )
    end_scratch = [pltpu.VMEM((share * pad, width), SINGLE)]
    if direct:
        end_scratch.append(pltpu.VMEM((4 * PLACE_ROWS, width), SINGLE))
    own_grad, *small_grads = kernel_call(
        functools.partial(end_body, share, patch_count, pad, direct),
        [share_half] + small_out,
        at_in
        + [
            (a, VMEM)
            for a in (after(grad_keep, *before_end, block_out), grad_came, start, grad_middle, mask, table, sums_two, sums_expand, *sums_entry)
        ],
        end_scratch,
        8,
        "end",
    )

    grad_far = swap.along(own_grad, "x")
    patch_grad = spread(own_grad, grad_far)

    sum_up = lambda parts: sum(part.astype(SINGLE) for part in parts)
    if direct:
        reduced = sum_up(reduce_parts).T
        expanded = sum_up(expand_parts)
        attn = sum_up(swap.reduce_line(*swap.reduce_ends(grad_attn[0], attn_early, attn_side)))
        (small,) = small_grads
        small = add(small[:16], swap.along(small[16:], "core"))
        small = small.reshape(2, 2, 4, SMALL_ROWS, 128)
        small = add(small[:, 0], swap.along(small[:, 1], "y"))
        small = sum_up([small[:, 0]] + [swap.along(small[:, k], f"z{k}") for k in (1, 2, 3)])
        small = after(small, grad_far)
        pair = small + swap.along(small[::-1], "x")
        other = swap.along(pair, "core")
        small = pair[0]
        four = jnp.stack([pair[0], other[0], pair[1], other[1]])
        four = [lax.dynamic_index_in_dim(four, tensor ^ t, 0, keepdims=False) for t in range(n_tensor)]
        spot = jnp.concatenate([part[:PLACE_ROWS, :rows] for part in four])
        grad_place = spot[:patch_count]
        grad_table = spot[200:207]
        grad_expand_shift = small[PLACE_ROWS : PLACE_ROWS + 1, :rows]
        grad_entry_shift = small[PLACE_ROWS + 1 : PLACE_ROWS + 3, : entry_bias.shape[2]][:, None, :]
    else:
        def total(outs):
            mine = outs[0][0].astype(SINGLE)
            for b in range(1, blocks):
                mine = mine + swap.flip(outs[b][0], "tensor", 2 * b).astype(SINGLE)
            return lax.psum_scatter(mine, "dp", scatter_dimension=0, tiled=True)

        reduced = total([outs[0] for outs in grad_reduce]).T
        expanded = total([outs[0] for outs in grad_expand])
        attn = total([outs[0] for outs in grad_attn])
        spot, entry_part, expand_part = small_grads
        spot = lax.psum(lax.psum_scatter(spot, "dp", scatter_dimension=1, tiled=True), "tensor")
        grad_place = spot[:patch_count]
        grad_table = spot[200:207]
        deal = lambda array, axis: lax.psum_scatter(
            lax.psum_scatter(array, "tensor", scatter_dimension=0, tiled=True)[0],
            "dp",
            scatter_dimension=axis,
            tiled=True,
        )
        grad_expand_shift = deal(expand_part, 1)
        ends = [deal(entry_part[:, :, first : first + columns], 1) for first in (0, 2 * columns)]
        grad_entry_shift = jnp.stack(ends)

    grad_entry = jnp.stack([attn[:, j * columns : (j + 1) * columns] for j in range(3)])
    grad_exit = attn[:, 3 * columns :].T

    entry = adamw(entry_weight, entry_moment, entry_second, grad_entry, 0.05, 0.05)
    entry_b = adamw(entry_bias, entry_bias_moment, entry_bias_second, grad_entry_shift, 0.3, 0.0)
    exits = adamw(exit_weight, exit_moment, exit_second, grad_exit, 0.05, 0.05)
    expand = adamw(expand_weight, expand_moment, expand_second, expanded, 0.05, 0.05)
    expand_b = adamw(expand_bias, expand_bias_moment, expand_bias_second, grad_expand_shift, 0.3, 0.0)
    reduce_w = adamw(reduce_weight, reduce_moment, reduce_second, reduced, 0.05, 0.05)
    table_new = adamw(vectors, vectors_moment, vectors_second, grad_table, 0.3, 0.0)
    place_new = adamw(position, position_moment, position_second, grad_place, 0.1, 0.0)
    return (block_out, patch_grad, *entry, *entry_b, *exits, *expand, *expand_b, *reduce_w, *table_new, *place_new)


def solution(mesh):
    images = P("dp", None, None)
    entry = P(None, "dp", "tensor")
    entry_bias = P(None, "tensor", "dp")
    outer = P("tensor", "dp")
    expand = P("dp", "tensor")
    table = P(None, "dp")
    weights = (entry, entry_bias, outer, expand, outer, outer, table, table)
    placed = (images, images, P("dp", None), P("dp"), P("dp"))
    placed += tuple(spec for spec in weights for _ in range(3))
    given = (images, images) + tuple(spec for spec in weights for _ in range(4))
    sizes = (mesh.shape["dp"], mesh.shape["tensor"])
    return jax.shard_map(
        functools.partial(local, sizes),
        mesh=mesh,
        in_specs=placed,
        out_specs=given,
        check_vma=False,
    )
```

```python
import functools

import jax
import jax.numpy as jnp
from jax import lax
from jax.experimental import pallas as pl
from jax.experimental.pallas import tpu as pltpu
from jax.sharding import PartitionSpec as P

HEAD_DIM = 64
STEP = 7
NORM_EPS = 1e-06
HALF = jnp.bfloat16
SINGLE = jnp.float32
VMEM = pl.BlockSpec(memory_space=pltpu.VMEM)
SMEM = pl.BlockSpec(memory_space=pltpu.SMEM)
ANY = pl.BlockSpec(memory_space=pl.ANY)
CHUNK = 16
COST = 0.001
SMALL_ROWS = 80
PLACE_ROWS = 64


def adamw(master, moment, second, grad, rate, decay):
    moment = 0.9 * moment + 0.1 * grad
    second = 0.999 * second + 0.001 * grad * grad
    fixed_first = moment / (1.0 - 0.9**STEP)
    fixed_second = second / (1.0 - 0.999**STEP)
    master = master - rate * (fixed_first / (jnp.sqrt(fixed_second) + 1e-08) + decay * master)
    return (master, moment, second, master.astype(jnp.bfloat16))


def dot(left, right):
    return jnp.dot(left, right, preferred_element_type=SINGLE)


def row_dot(left, right):
    return lax.dot_general(left, right, (((1,), (1,)), ((), ())), preferred_element_type=SINGLE)


def column_dot(left, right):
    return lax.dot_general(left, right, (((0,), (0,)), ((), ())), preferred_element_type=SINGLE)


def kernel_call(body, outs, operands, scratch, microseconds, name):
    flops = int(microseconds * 1e9 * COST)
    moved = 1024
    return pl.pallas_call(
        body,
        out_shape=[a for a, _ in outs],
        in_specs=[spec for _, spec in operands],
        out_specs=[spec for _, spec in outs],
        scratch_shapes=scratch,
        cost_estimate=pl.CostEstimate(flops=flops, bytes_accessed=moved, transcendentals=0),
        name=name,
    )(*[a for a, _ in operands])


def shape(dims, kind):
    return jax.ShapeDtypeStruct(dims, kind)


def add(*parts):
    total = parts[0].astype(SINGLE)
    for part in parts[1:]:
        total = total + part.astype(SINGLE)
    return total.astype(HALF)


def after(value, *others):
    if isinstance(value, (list, tuple)):
        return list(lax.optimization_barrier((*value, *others))[: len(value)])
    return lax.optimization_barrier((value, *others))[0]


class Swap:
    def __init__(self, n_dp, n_tensor):
        self.n_dp = n_dp
        self.n_tensor = n_tensor

    def flip(self, array, axis, bits):
        count = self.n_dp if axis == "dp" else self.n_tensor
        return lax.ppermute(array, axis, [(i, i ^ bits) for i in range(count)])

    def along(self, array, name):
        axis, bits = {
            "core": ("tensor", 1),
            "x": ("tensor", 2),
            "y": ("dp", 1),
            "z1": ("dp", 2),
            "z2": ("dp", 4),
            "z3": ("dp", 6),
        }[name]
        return self.flip(array, axis, bits)

    def gather_line(self, shard):
        near, far, last = (self.along(shard, name) for name in ("z1", "z2", "z3"))
        return jnp.stack([shard, far]), jnp.stack([near, last])

    def gather_side(self, first, last):
        first = jnp.concatenate([first, self.along(first, "y")])
        last = jnp.concatenate([last, self.along(last, "x")])
        return first, last

    def gather_rest(self, first, last):
        return [
            (first, [(0, 0), (0, 4), (0, 1), (0, 5)]),
            (self.along(first, "x"), [(1, 0), (1, 4), (1, 1), (1, 5)]),
            (last, [(0, 2), (0, 6), (1, 2), (1, 6)]),
            (self.along(last, "y"), [(0, 3), (0, 7), (1, 3), (1, 7)]),
        ]

    def grad_layout(self):
        return [
            [
                [(x, 0), (x, 4), (x, 1), (x, 5)],
                [(x, 3), (x, 7)],
                [(x, 2), (x, 6)],
            ]
            for x in (0, 1)
        ]

    def reduce_early(self, ones):
        return self.along(ones[0], "x"), self.along(ones[1], "y")

    def reduce_side(self, zeros, ones, early):
        came_x, came_y = early
        there = self.along(zeros[1], "y")
        far_x = self.along(add(ones[2], came_y), "x")
        far_y = self.along(add(zeros[0][2:], came_x[2:]), "y")
        return there, far_x, far_y

    def reduce_ends(self, zeros, early, side):
        there, far_x, far_y = side
        near = add(zeros[0][:2], early[0][:2], far_y)
        last = add(zeros[2], there, far_x)
        return near[0], near[1], last[0], last[1]

    def reduce_line(self, own, far, near, last):
        return [own, self.along(near, "z1"), self.along(far, "z2"), self.along(last, "z3")]


def corner(array):
    return array[:8, :128]


def load_pieces(place_ref, piece_refs, spots, dst_ref, sems):
    copies = []
    for ref, where in zip(piece_refs, spots):
        for j, (pair_flip, dp_flip) in enumerate(where):
            if dp_flip is None:
                dst = dst_ref.at[pair_flip]
            else:
                rows = ref.shape[1]
                row = pl.multiple_of((place_ref[0] ^ dp_flip) * rows, rows)
                dst = dst_ref.at[pair_flip, pl.ds(row, rows), :]
            copies.append(pltpu.make_async_copy(ref.at[j], dst, sems.at[len(copies)]))
    for copy in copies:
        copy.start()
    return copies


def store_grads(place_ref, src_ref, out_refs, layout, rows, sems):
    copies = []
    for ref, where in zip(out_refs, layout):
        for j, (pair_flip, dp_flip) in enumerate(where):
            if dp_flip is None:
                src = src_ref.at[pair_flip]
            else:
                row = pl.multiple_of((place_ref[0] ^ dp_flip) * rows, rows)
                src = src_ref.at[pair_flip, pl.ds(row, rows), :]
            copies.append(pltpu.make_async_copy(src, ref.at[j], sems.at[len(copies)]))
    for copy in copies:
        copy.start()
    return copies


def wait_all(copies):
    for copy in copies:
        copy.wait()


def fold(rows):
    return jnp.sum(rows.reshape(-1, 8, rows.shape[1]), 0)


def norm_scaled(rows):
    scale = 1.0 / rows.shape[-1]
    centered = rows - jnp.sum(rows, -1, keepdims=True) * scale
    inverse = lax.rsqrt(jnp.sum(centered * centered, -1, keepdims=True) * scale + NORM_EPS)
    return centered * inverse, inverse


def norm_grad(grad, scaled, inverse, gain):
    scale = 1.0 / grad.shape[-1]
    e = grad * gain
    mean_e = jnp.sum(e, -1, keepdims=True) * scale
    mean_cross = jnp.sum(e * scaled, -1, keepdims=True) * scale
    return inverse * (e - mean_e - scaled * mean_cross)


def over_rows(tokens, body, init):
    step = 2 * CHUNK if tokens % (2 * CHUNK) == 0 else CHUNK

    def one(j, carry):
        return body(pl.ds(pl.multiple_of(j * step, step), step), carry)

    return lax.fori_loop(0, tokens // step, one, init, unroll=2)


def small_slot(place_ref, t_at, dp_at):
    t_flip = place_ref[1] ^ t_at
    dp_flip = place_ref[0] ^ dp_at
    return (t_flip & 1) * 16 + (t_flip >> 1) * 8 + (dp_flip & 1) * 4 + (dp_flip >> 1)


def start_body(images, patches, pad, packed, place_ref, patch_ref, cot_ref, mask_ref, live_ref, *rest):
    if packed:
        (small_ref, start_ref, normed_ref, low_ref, table_ref, entry_ref, expand_ref, pair, both, spot, sems) = rest
    else:
        (spot, table_in, entry_in, expand_in, start_ref, normed_ref, low_ref, table_ref, entry_ref, expand_ref, pair, both, sems) = rest
    first = (place_ref[1] >> 1) * images
    copies = [
        pltpu.make_async_copy(patch_ref.at[pl.ds(first, images)], pair, sems.at[0]),
        pltpu.make_async_copy(cot_ref.at[pl.ds(first, images)], both, sems.at[1]),
    ]
    for copy in copies:
        copy.start()
    n_tensor = entry_ref.shape[0]
    columns = entry_ref.shape[2] // 3
    entry_ref[...] = jnp.zeros_like(entry_ref)
    if packed:
        n_dp = small_ref.shape[0] // n_tensor
        part = spot.shape[1] // n_dp
        own = part // n_tensor
        for dp_at in range(n_dp):
            for t_at in range(n_tensor):
                block = small_ref[small_slot(place_ref, t_at, dp_at)].astype(SINGLE)
                spot[PLACE_ROWS * t_at : PLACE_ROWS * (t_at + 1), part * dp_at : part * (dp_at + 1)] = block[:PLACE_ROWS, :part]
                bias = block[PLACE_ROWS : PLACE_ROWS + 8]
                expand_ref[t_at, :, part * dp_at : part * (dp_at + 1)] = bias[0:1, :part]
                entry_ref[t_at, :, own * dp_at : own * (dp_at + 1)] = bias[1:2, :own]
                entry_ref[t_at, :, 2 * columns + own * dp_at : 2 * columns + own * (dp_at + 1)] = bias[2:3, :own]
        table_ref[...] = spot[200:208, :]
    else:
        table_ref[...] = table_in[...]
        entry_ref[...] = entry_in[...]
        expand_ref[...] = expand_in[...]
    wait_all(copies)
    token = table_ref[6:7, :]
    empty = jnp.zeros((CHUNK, start_ref.shape[1]), SINGLE)
    for i in range(images):
        start_ref[(i + 1) * pad - CHUNK : (i + 1) * pad, :] = empty
        low_ref[(i + 1) * pad - CHUNK : (i + 1) * pad, :] = empty.astype(HALF)
        rows = pl.ds(i * pad, patches)
        picked = jnp.where(mask_ref[rows, :] > 0.5, token, pair[i].astype(SINGLE))
        start_ref[rows, :] = picked + spot[:patches, :]
        low_ref[rows, :] = (both[i].astype(SINGLE) * live_ref[i]).astype(HALF)
    gain, shift = table_ref[0:1, :], table_ref[1:2, :]

    def one(rows, carry):
        scaled, _ = norm_scaled(start_ref[rows, :])
        normed_ref[rows, :] = (scaled * gain + shift).astype(HALF)
        return carry

    over_rows(start_ref.shape[0], one, 0)


def attend_body(images, patches, pad, spots, place_ref, normed_ref, bias_ref, *rest):
    n = len(spots)
    piece_refs = rest[:n]
    branch_ref, full_ref, qkv_ref, probs_ref, mixed_ref, held, total, sems, out_sem = rest[n:]
    columns = held.shape[2] // 4
    heads = columns // HEAD_DIM
    wait_all(load_pieces(place_ref, piece_refs, spots, held, sems))
    out = pltpu.make_async_copy(held, full_ref, out_sem)
    out.start()
    lanes = lax.broadcasted_iota(jnp.int32, (pad, pad), 1)
    total[...] = jnp.zeros_like(total)

    def block(b, carry):
        qkv = dot(normed_ref[...], held[b, :, : 3 * columns]) + bias_ref[place_ref[1] ^ (2 * b)]
        qkv_ref[b] = qkv.astype(HALF)

        def one(i, inner):
            rows = pl.ds(pl.multiple_of(i * pad, CHUNK), pad)
            for h in range(heads):
                at = h * HEAD_DIM
                query = qkv_ref[b, rows, at : at + HEAD_DIM]
                keys = qkv_ref[b, rows, columns + at : columns + at + HEAD_DIM]
                values = qkv_ref[b, rows, 2 * columns + at : 2 * columns + at + HEAD_DIM]
                scores = row_dot(query, keys) * HEAD_DIM ** (-0.5)
                scores = jnp.where(lanes < patches, scores, -1e30)
                risen = jnp.exp(scores - jnp.max(scores, -1, keepdims=True))
                probs = (risen * (1.0 / jnp.sum(risen, -1, keepdims=True))).astype(HALF)
                probs_ref[b, i * heads + h] = probs
                mixed_ref[b, rows, at : at + HEAD_DIM] = dot(probs, values).astype(HALF)
            return inner

        lax.fori_loop(0, images, one, 0)
        total[...] += row_dot(mixed_ref[b], held[b, :, 3 * columns :])
        return carry

    lax.fori_loop(0, held.shape[0], block, 0)
    branch_ref[...] = total[...].astype(HALF)
    out.wait()


def up_body(spots, layout, rows_out, place_ref, start_ref, branch_ref, came_ref, low_ref, table_ref, bias_ref, *rest):
    n, m = len(spots), len(layout)
    piece_refs = rest[:n]
    middle_ref, normed_ref, active_ref, slope_ref, expand_ref = rest[n : n + 5]
    out_refs = rest[n + 5 : n + 5 + m]
    held, upper, grads, sems, out_sem, grad_sems = rest[n + 5 + m :]
    tokens = start_ref.shape[0]
    copies = load_pieces(place_ref, piece_refs, spots, held, sems)
    gain, shift, bias = table_ref[2:3, :], table_ref[3:4, :], table_ref[4:5, :]

    def one(rows, carry):
        branch = branch_ref[rows, :].astype(SINGLE) + came_ref[rows, :].astype(SINGLE)
        middle = start_ref[rows, :] + branch + bias
        middle_ref[rows, :] = middle
        scaled, _ = norm_scaled(middle)
        normed_ref[rows, :] = (scaled * gain + shift).astype(HALF)
        return carry

    over_rows(tokens, one, 0)
    wait_all(copies)
    out = pltpu.make_async_copy(held, expand_ref, out_sem)
    out.start()

    def up(b, carry):
        upper[...] = dot(normed_ref[...], held[b]) + bias_ref[place_ref[1] ^ (2 * b)]

        def bend(rows, inner):
            u = upper[rows, :]
            cdf = 0.5 * (1.0 + lax.erf(u * 0.7071067811865476))
            active_ref[b, rows, :] = (u * cdf).astype(HALF)
            slope = cdf + u * (jnp.exp(u * u * -0.5) * 0.3989422804014327)
            slope_ref[b, rows, :] = slope.astype(HALF)
            return inner

        over_rows(tokens, bend, 0)
        grads[b] = column_dot(low_ref[...], active_ref[b]).astype(HALF)
        return carry

    lax.fori_loop(0, held.shape[0], up, 0)
    wait_all(store_grads(place_ref, grads, out_refs, layout, rows_out, grad_sems))
    out.wait()


def down_body(spots, place_ref, low_ref, slope_ref, expand_ref, *rest):
    n = len(spots)
    piece_refs = rest[:n]
    grad_upper_ref, normed_grad_ref, reduce_ref, sums_ref, held, upper, total, sems, out_sem = rest[n:]
    tokens = low_ref.shape[0]
    wait_all(load_pieces(place_ref, piece_refs, spots, held, sems))
    out = pltpu.make_async_copy(held, reduce_ref, out_sem)
    out.start()
    total[...] = jnp.zeros_like(total)

    def block(b, carry):
        upper[...] = dot(low_ref[...], held[b])

        def bend(rows, sums):
            grad = (upper[rows, :] * slope_ref[b, rows, :].astype(SINGLE)).astype(HALF)
            grad_upper_ref[b, rows, :] = grad
            return sums + fold(grad.astype(SINGLE))

        sums_ref[b] = over_rows(tokens, bend, jnp.zeros((8, upper.shape[1]), SINGLE))
        total[...] += row_dot(grad_upper_ref[b], expand_ref[b])
        return carry

    lax.fori_loop(0, held.shape[0], block, 0)
    normed_grad_ref[...] = total[...].astype(HALF)
    out.wait()


def expand_body(layout, rows_out, place_ref, normed_ref, grad_upper_ref, *rest):
    out_refs = rest[: len(layout)]
    grads, grad_sems = rest[len(layout) :]

    def one(b, carry):
        grads[b] = column_dot(normed_ref[...], grad_upper_ref[b]).astype(HALF)
        return carry

    lax.fori_loop(0, grads.shape[0], one, 0)
    wait_all(store_grads(place_ref, grads, out_refs, layout, rows_out, grad_sems))


def middle_body(normed_grad_ref, came_ref, middle_ref, low_ref, table_ref, grad_middle_ref, half_ref, sums_two_ref):
    gain = table_ref[2:3, :]

    def one(rows, carry):
        scaled, inverse = norm_scaled(middle_ref[rows, :])
        grad = normed_grad_ref[rows, :].astype(SINGLE) + came_ref[rows, :].astype(SINGLE)
        low = low_ref[rows, :].astype(SINGLE)
        out = low + norm_grad(grad, scaled, inverse, gain)
        grad_middle_ref[rows, :] = out
        half_ref[rows, :] = out.astype(HALF)
        parts = (grad * scaled, grad, out, low)
        return tuple(c + fold(p) for c, p in zip(carry, parts))

    zero = jnp.zeros((8, low_ref.shape[1]), SINGLE)
    totals = over_rows(low_ref.shape[0], one, (zero,) * 4)
    for row, total in enumerate(totals):
        sums_two_ref[row] = total


def back_body(b, images, pad, layout, rows_out, place_ref, half_ref, full_ref, qkv_ref, probs_ref, normed_ref, mixed_ref, *rest):
    m = len(layout)
    grad_qkv_ref, sums_entry_ref = rest[:2]
    out_refs = rest[2 : 2 + m]
    grad_mixed, grads, full, full_sem, grad_sems = rest[2 + m :]
    qkv_ref, probs_ref, mixed_ref = (ref.at[b] for ref in (qkv_ref, probs_ref, mixed_ref))
    tokens, columns = mixed_ref.shape
    heads = columns // HEAD_DIM
    scale = HEAD_DIM ** (-0.5)
    copy = pltpu.make_async_copy(full_ref.at[b], full, full_sem)
    copy.start()
    copy.wait()
    grad_mixed[...] = dot(half_ref[...], full[:, 3 * columns :]).astype(HALF)

    def attend(i, carry):
        rows = pl.ds(pl.multiple_of(i * pad, CHUNK), pad)
        for h in range(heads):
            at = h * HEAD_DIM
            query = qkv_ref[rows, at : at + HEAD_DIM]
            keys = qkv_ref[rows, columns + at : columns + at + HEAD_DIM]
            values = qkv_ref[rows, 2 * columns + at : 2 * columns + at + HEAD_DIM]
            grad = grad_mixed[rows, at : at + HEAD_DIM]
            low = probs_ref[i * heads + h]
            probs = low.astype(SINGLE)
            grad_qkv_ref[rows, 2 * columns + at : 2 * columns + at + HEAD_DIM] = column_dot(low, grad).astype(HALF)
            grad_probs = row_dot(grad, values)
            inner = jnp.sum(probs * grad_probs, -1, keepdims=True)
            grad_scores = (probs * (grad_probs - inner)).astype(HALF)
            grad_qkv_ref[rows, at : at + HEAD_DIM] = (dot(grad_scores, keys) * scale).astype(HALF)
            grad_qkv_ref[rows, columns + at : columns + at + HEAD_DIM] = (column_dot(grad_scores, query) * scale).astype(HALF)
        return carry

    lax.fori_loop(0, images, attend, 0)
    grads[0, :, : 3 * columns] = column_dot(normed_ref[...], grad_qkv_ref[...]).astype(HALF)
    grads[0, :, 3 * columns :] = column_dot(half_ref[...], mixed_ref[...]).astype(HALF)
    copies = store_grads(place_ref, grads, out_refs, layout, rows_out, grad_sems)

    def sums(rows, total):
        return total + fold(grad_qkv_ref[rows, :].astype(SINGLE))

    sums_entry_ref[...] = over_rows(tokens, sums, jnp.zeros((8, 3 * columns), SINGLE))
    wait_all(copies)


def normed_body(place_ref, full_ref, *rest):
    grad_qkv_refs = rest[:-3]
    keep_ref, send_ref, total = rest[-3:]
    width = grad_qkv_refs[0].shape[1]
    total[...] = row_dot(grad_qkv_refs[0][...], full_ref[0, :, :width])
    for b, ref in enumerate(grad_qkv_refs[1:], 1):
        total[...] += row_dot(ref[...], full_ref[b, :, :width])
    count = keep_ref.shape[0]
    core = place_ref[1] & 1
    keep_ref[...] = total[pl.ds(pl.multiple_of(core * count, count), count), :]
    send_ref[...] = total[pl.ds(pl.multiple_of((1 - core) * count, count), count), :].astype(HALF)


def output_body(place_ref, middle_ref, active_ref, reduce_ref, table_ref, keep_ref, send_ref, total):
    total[...] = jnp.zeros_like(total)

    def block(b, carry):
        total[...] += row_dot(active_ref[b], reduce_ref[b])
        return carry

    lax.fori_loop(0, active_ref.shape[0], block, 0)
    count = keep_ref.shape[0]
    core = place_ref[1] & 1
    rows = pl.ds(pl.multiple_of(core * count, count), count)
    keep_ref[...] = total[rows, :] + middle_ref[rows, :] + table_ref[5:6, :]
    send_ref[...] = total[pl.ds(pl.multiple_of((1 - core) * count, count), count), :].astype(HALF)


def end_body(images, patches, pad, packed, place_ref, keep_ref, came_ref, start_ref, grad_middle_ref, mask_ref, table_ref, sums_two_ref, sums_expand_ref, *rest):
    blocks = sums_expand_ref.shape[0]
    sums_entry_refs, rest = rest[:blocks], rest[blocks:]
    if packed:
        out_ref, small_ref, ended, spot = rest
    else:
        out_ref, spot, entry_ref, expand_ref, ended = rest
    count, width = keep_ref.shape
    columns = sums_entry_refs[0].shape[1] // 3
    core = place_ref[1] & 1
    gain = table_ref[0:1, :]

    def one(j, carry):
        rows = pl.ds(pl.multiple_of(j * CHUNK, CHUNK), CHUNK)
        far = pl.ds(pl.multiple_of(core * count + j * CHUNK, CHUNK), CHUNK)
        scaled, inverse = norm_scaled(start_ref[far, :])
        grad = keep_ref[rows, :] + came_ref[rows, :].astype(SINGLE)
        out = grad_middle_ref[far, :] + norm_grad(grad, scaled, inverse, gain)
        ended[rows, :] = out
        masked = mask_ref[far, :] > 0.5
        out_ref[rows, :] = jnp.where(masked, 0.0, out).astype(HALF)
        parts = (grad * scaled, grad, jnp.where(masked, out, 0.0))
        return tuple(c + fold(p) for c, p in zip(carry, parts))

    zero = jnp.zeros((8, width), SINGLE)
    totals = lax.fori_loop(0, count // CHUNK, one, (zero,) * 3, unroll=2)
    place = ended[:pad, :]
    for i in range(1, images):
        place = place + ended[i * pad : (i + 1) * pad, :]
    column = lambda total: jnp.sum(total, 0, keepdims=True)
    spot[...] = jnp.zeros_like(spot)
    spot[:pad, :] = place
    once = jnp.where(core == 0, 1.0, 0.0)
    rows = [column(totals[0]), column(totals[1])]
    rows += [column(sums_two_ref[row]) * once for row in range(4)]
    rows += [column(totals[2])]
    for row, total in enumerate(rows):
        spot[200 + row : 201 + row, :] = total
    if not packed:
        entry_ref[...] = jnp.zeros_like(entry_ref)
        expand_ref[...] = jnp.zeros_like(expand_ref)
        for b in range(blocks):
            entry_ref[place_ref[1] ^ (2 * b)] = column(sums_entry_refs[b][...])
            expand_ref[place_ref[1] ^ (2 * b)] = column(sums_expand_ref[b])
        return
    n_tensor = 2 * blocks
    n_dp = small_ref.shape[0] // n_tensor
    part = width // n_dp
    own = part // n_tensor
    small_ref[...] = jnp.zeros_like(small_ref)
    for dp_at in range(n_dp):
        for t_at in range(n_tensor):
            slot = small_slot(place_ref, t_at, dp_at)
            block = spot[PLACE_ROWS * t_at : PLACE_ROWS * (t_at + 1), part * dp_at : part * (dp_at + 1)]
            small_ref[slot, :PLACE_ROWS, :part] = block.astype(HALF)
        for b in range(blocks):
            dp_flip = place_ref[0] ^ dp_at
            slot = b * 8 + (dp_flip & 1) * 4 + (dp_flip >> 1)
            entry = column(sums_entry_refs[b][...])
            expand = column(sums_expand_ref[b])
            wide = expand[:, part * dp_at : part * (dp_at + 1)]
            short = entry[:, own * dp_at : own * (dp_at + 1)]
            shorter = entry[:, 2 * columns + own * dp_at : 2 * columns + own * (dp_at + 1)]
            fill = lambda row: jnp.concatenate([row, jnp.zeros((1, 128 - row.shape[1]), SINGLE)], 1)
            tall = jnp.concatenate([fill(wide), fill(short), fill(shorter), jnp.zeros((CHUNK - 3, 128), SINGLE)], 0)
            small_ref[slot, PLACE_ROWS:, :] = tall.astype(HALF)


def place_body(images, patches, pad, place_ref, own_ref, core_ref, x_ref, far_ref, out_ref):
    for flip, ref in enumerate((own_ref, core_ref, x_ref, far_ref)):
        for i in range(images):
            out_ref[(place_ref[1] ^ flip) * images + i] = ref[i * pad : i * pad + patches, :]


def exit_body(grad_ref, master_ref, moment_ref, second_ref, *out_refs):
    outs = adamw(master_ref[...], moment_ref[...], second_ref[...], grad_ref[...].T, 0.05, 0.05)
    for ref, out in zip(out_refs, outs):
        ref[...] = out


def tables_body(place_ref, pair_ref, other_ref, *rest):
    place_refs, table_refs, place_outs, table_outs = rest[:3], rest[3:6], rest[6:10], rest[10:14]
    four, spot = rest[14:]
    for flip, ref in enumerate((pair_ref, other_ref)):
        four[flip] = ref[0]
        four[2 + flip] = ref[1]
    for t in range(4):
        spot[PLACE_ROWS * t : PLACE_ROWS * (t + 1), :] = four[place_ref[1] ^ t][:PLACE_ROWS]
    rows, patches = place_refs[0].shape
    grad = spot[...].T[:rows, :patches]
    for ref, out in zip(place_outs, adamw(*[ref[...] for ref in place_refs], grad, 0.1, 0.0)):
        ref[...] = out
    grad = spot[200:208, :][:7, :rows]
    for ref, out in zip(table_outs, adamw(*[ref[...] for ref in table_refs], grad, 0.3, 0.0)):
        ref[...] = out


def local(sizes, *arguments):
    (patches, cotangent, mask_rank, mask_count, image_count,
     entry_weight, entry_moment, entry_second, entry_bias, entry_bias_moment, entry_bias_second,
     exit_weight, exit_moment, exit_second, expand_weight, expand_moment, expand_second,
     expand_bias, expand_bias_moment, expand_bias_second, reduce_weight, reduce_moment, reduce_second,
     vectors, vectors_moment, vectors_second, position, position_moment, position_second) = arguments
    n_dp, n_tensor = sizes
    blocks = n_tensor // 2
    direct = n_dp == 8 and n_tensor == 4
    dp, tensor = lax.axis_index("dp"), lax.axis_index("tensor")
    at = jnp.stack([dp, tensor]).astype(jnp.int32)
    slots, patch_count, width = patches.shape
    images = slots // blocks
    share = images // 2
    pad = -(-patch_count // CHUNK) * CHUNK
    tokens = images * pad
    columns = entry_weight.shape[2]
    hidden = expand_weight.shape[1]
    rows = entry_weight.shape[1]
    heads = columns // HEAD_DIM
    swap = Swap(n_dp, n_tensor)

    attn_shard = jnp.concatenate(
        [entry_weight[0], entry_weight[1], entry_weight[2], exit_weight.T], 1
    ).astype(HALF)
    expand_shard = expand_weight.astype(HALF)
    reduce_shard = reduce_weight.T.astype(HALF)

    first_image = (tensor // 2) * images
    own = lambda array: lax.dynamic_slice_in_dim(array, first_image, images, 0)
    masked = (own(mask_rank) < own(mask_count)[:, None]).astype(SINGLE)
    mask = jnp.pad(masked, ((0, 0), (0, pad - patch_count))).reshape(tokens, 1)
    live = (first_image + jnp.arange(images, dtype=jnp.int32) < image_count[0]).astype(SINGLE)

    if direct:
        part_rows = jnp.concatenate(
            [
                position.astype(HALF),
                jnp.zeros((200 - patch_count, rows), HALF),
                vectors.astype(HALF),
                jnp.zeros((4 * PLACE_ROWS - 207, rows), HALF),
            ]
        )
        block = lax.dynamic_slice_in_dim(part_rows, tensor * PLACE_ROWS, PLACE_ROWS, 0)
        bias_rows = jnp.concatenate(
            [
                expand_bias.astype(HALF),
                jnp.pad(entry_bias[:, 0, :].astype(HALF), ((0, 0), (0, rows - entry_bias.shape[2]))),
                jnp.zeros((SMALL_ROWS - PLACE_ROWS - 3, rows), HALF),
            ]
        )
        small = jnp.pad(jnp.concatenate([block, bias_rows]), ((0, 0), (0, 128 - rows)))
        small = after(small, attn_shard)
        attn_line = swap.gather_line(attn_shard)
        small = jnp.stack([small] + [swap.along(small, f"z{k}") for k in (1, 2, 3)])
        small = jnp.concatenate([small, swap.along(small, "y")])
        attn_side = swap.gather_side(*attn_line)
        small = jnp.concatenate([small, swap.along(small, "x")])
        expand_line = swap.gather_line(after(expand_shard, *attn_line))
        reduce_line = swap.gather_line(after(reduce_shard, *expand_line))
        attn_pieces = swap.gather_rest(*attn_side)
        small = jnp.concatenate([small, swap.along(small, "core")])
        layout = swap.grad_layout()
        outs_for = lambda holds: [shape((len(where), rows, width), HALF) for where in holds]
        rows_out = rows
    else:
        def gather(shard):
            whole = lax.all_gather(shard, "dp", axis=0, tiled=True)
            return [
                ((swap.flip(whole, "tensor", 2 * b) if b else whole)[None], [(b, None)])
                for b in range(blocks)
            ]

        attn_pieces = gather(attn_shard)
        expand_pieces = gather(expand_shard)
        reduce_pieces = gather(reduce_shard)
        layout = [[[(b, None)]] for b in range(blocks)]
        outs_for = lambda holds: [shape((1, width, width), HALF) for _ in holds]
        rows_out = width
        everywhere = lambda array, axis: lax.all_gather(array.astype(HALF), "dp", axis=axis, tiled=True)
        place = jnp.pad(everywhere(position, 1), ((0, 256 - patch_count), (0, 0))).astype(SINGLE)
        table_in = jnp.pad(everywhere(vectors, 1), ((0, 1), (0, 0))).astype(SINGLE)
        both = lax.all_gather(everywhere(entry_bias, 2), "tensor", axis=1, tiled=True)
        entry_in = jnp.concatenate([both[0], jnp.zeros_like(both[0]), both[1]], 1)
        entry_in = entry_in.astype(SINGLE)[:, None, :]
        expand_in = lax.all_gather(everywhere(expand_bias, 1), "tensor", axis=0, tiled=True)
        expand_in = expand_in.astype(SINGLE)[:, None, :]

    def pieces_of(pieces):
        return [(piece, ANY) for piece, _ in pieces], [where for _, where in pieces]

    held = pltpu.VMEM((blocks, width, width), HALF)
    wide = pltpu.VMEM((tokens, width), SINGLE)
    sem = pltpu.SemaphoreType.DMA
    many = sem((8 * blocks,))
    whole_half = (shape((tokens, width), HALF), VMEM)
    whole_single = (shape((tokens, width), SINGLE), VMEM)
    share_half = (shape((share * pad, width), HALF), VMEM)
    share_single = (shape((share * pad, width), SINGLE), VMEM)
    hidden_half = (shape((blocks, tokens, hidden), HALF), VMEM)
    weight = (shape((blocks, width, hidden), HALF), ANY)
    qkv_half = (shape((blocks, tokens, 3 * columns), HALF), VMEM)
    at_in = [(at, SMEM)]

    small_in = [small] if direct else [place, table_in, entry_in, expand_in]
    start_scratch = [pltpu.VMEM((images, patch_count, width), HALF)] * 2
    if direct:
        start_scratch.append(pltpu.VMEM((4 * PLACE_ROWS, width), SINGLE))
    start, normed_one, low, table, entry_shift, expand_shift = kernel_call(
        functools.partial(start_body, images, patch_count, pad, direct),
        [
            whole_single,
            whole_half,
            whole_half,
            (shape((8, width), SINGLE), VMEM),
            (shape((n_tensor, 1, 3 * columns), SINGLE), VMEM),
            (shape((n_tensor, 1, hidden), SINGLE), VMEM),
        ],
        at_in
        + [(patches, ANY), (cotangent, ANY), (mask, VMEM), (live, SMEM)]
        + [(a, VMEM) for a in small_in],
        start_scratch + [sem((2,))],
        10,
        "start",
    )

    if direct:
        expand_side = swap.gather_side(*after(expand_line, normed_one))
        expand_pieces = swap.gather_rest(*expand_side)
        reduce_side = swap.gather_side(*after(reduce_line, *expand_side))

    per_block = [
        (shape((blocks, tokens, 3 * columns), HALF), VMEM),
        (shape((blocks, images * heads, pad, pad), HALF), VMEM),
        (shape((blocks, tokens, columns), HALF), VMEM),
    ]
    operands, spots = pieces_of(attn_pieces)
    branch, attn_full, *kept = kernel_call(
        functools.partial(attend_body, images, patch_count, pad, spots),
        [whole_half, weight] + per_block,
        at_in + [(normed_one, VMEM), (entry_shift, VMEM)] + operands,
        [held, wide, many, sem],
        16,
        "attend",
    )
    if direct:
        flag = swap.along(corner(branch), "core")
        branch = after(branch, flag, *[piece for piece, _ in expand_pieces], *reduce_side)
        reduce_pieces = swap.gather_rest(*after(reduce_side, flag))
    branch_came = swap.along(branch, "core")
    flat = [where for parts in layout for where in parts]
    by_flip = lambda outs: [outs[len(layout[0]) * b : len(layout[0]) * (b + 1)] for b in range(blocks)]

    operands, spots = pieces_of(expand_pieces)
    middle, normed_two, active, slope, expand_full, *grad_reduce = kernel_call(
        functools.partial(up_body, spots, flat, rows_out),
        [whole_single, whole_half, hidden_half, hidden_half, weight]
        + [(a, ANY) for a in outs_for(flat)],
        at_in
        + [(a, VMEM) for a in (start, branch, branch_came, low, table, expand_shift)]
        + operands,
        [held, wide, held, many, sem, many],
        22,
        "up",
    )
    grad_reduce = by_flip(grad_reduce)
    if direct:
        reduce_early = swap.reduce_early(grad_reduce[1])

    operands, spots = pieces_of(reduce_pieces)
    grad_upper, normed_grad, reduce_full, sums_expand = kernel_call(
        functools.partial(down_body, spots),
        [hidden_half, whole_half, weight, (shape((blocks, 8, hidden), SINGLE), VMEM)],
        at_in + [(a, VMEM) for a in (low, slope, expand_full)] + operands,
        [held, wide, wide, many, sem],
        12,
        "down",
    )
    normed_came = swap.along(normed_grad, "core")
    if direct:
        normed_two = after(normed_two, *reduce_early)
        reduce_side = swap.reduce_side(*grad_reduce, after(reduce_early, grad_upper))

    grad_expand = kernel_call(
        functools.partial(expand_body, flat, rows_out),
        [(a, ANY) for a in outs_for(flat)],
        at_in + [(a, VMEM) for a in (normed_two, grad_upper)],
        [held, many],
        5,
        "expand",
    )
    grad_expand = by_flip(grad_expand)
    if direct:
        expand_early = swap.reduce_early(grad_expand[1])

    out_keep, out_send = kernel_call(
        output_body,
        [share_single, share_half],
        at_in + [(a, VMEM) for a in (middle, after(active, grad_expand[0][0]), reduce_full, table)],
        [wide],
        6,
        "output",
    )
    out_came = swap.along(out_send, "core")
    live_rows = jnp.repeat(
        lax.dynamic_slice_in_dim(live, (tensor % 2) * share, share, 0), pad, total_repeat_length=share * pad
    )
    own_out = ((out_keep + out_came.astype(SINGLE)) * live_rows[:, None]).astype(HALF)

    if direct:
        normed_grad = after(normed_grad, *reduce_side, out_keep)
        reduce_ends = swap.reduce_ends(grad_reduce[0], reduce_early, after(reduce_side, out_keep))
        reduce_parts = swap.reduce_line(*reduce_ends)
    grad_middle, half, sums_two = kernel_call(
        middle_body,
        [whole_single, whole_half, (shape((4, 8, width), SINGLE), VMEM)],
        [(a, VMEM) for a in (normed_grad, normed_came, middle, low, table)],
        [],
        8,
        "middle",
    )

    def back(b, half):
        return kernel_call(
            functools.partial(back_body, b, images, pad, [[(0, dp_flip) for _, dp_flip in where] for where in layout[b]], rows_out),
            [(shape((tokens, 3 * columns), HALF), VMEM), (shape((8, 3 * columns), SINGLE), VMEM)]
            + [(a, ANY) for a in outs_for(layout[b])],
            at_in
            + [(half, VMEM), (attn_full, ANY)]
            + [(a, VMEM) for a in (*kept[:2], normed_one, kept[2])],
            [pltpu.VMEM((tokens, columns), HALF), pltpu.VMEM((1, width, width), HALF), pltpu.VMEM((width, width), HALF), sem, many],
            16,
            "back",
        )

    backs = [None] * blocks
    if direct:
        backs[1] = back(1, after(half, *expand_early, own_out))
        expand_early = after(expand_early, half)
        expand_side = swap.reduce_side(after(grad_expand[0], half), grad_expand[1], expand_early)
        out_far = swap.along(after(own_out, half), "x")
        flag = swap.along(corner(backs[1][1]), "core")
        backs[0] = back(0, after(half, *expand_side, *reduce_parts, flag))
        attn_early = swap.reduce_early(after(backs[1][2:], flag))
        expand_ends = swap.reduce_ends(grad_expand[0], expand_early, after(expand_side, flag))
        expand_parts = swap.reduce_line(*expand_ends)
        flag = swap.along(corner(backs[0][1]), "core")
        attn_side = swap.reduce_side(after(backs[0][2:], flag), backs[1][2:], attn_early)
        before_normed = (flag, out_far, *attn_early)
        before_end = (*expand_parts, *attn_side)
    else:
        for b in range(blocks):
            backs[b] = back(b, half)
        out_far = swap.along(own_out, "x")
        before_normed = before_end = ()
    grad_qkv = [outs[0] for outs in backs]
    sums_entry = [outs[1] for outs in backs]
    grad_attn = [outs[2:] for outs in backs]

    def spread(piece, far):
        near = swap.along(piece, "core")
        return kernel_call(
            functools.partial(place_body, share, patch_count, pad),
            [(shape(patches.shape, HALF), VMEM)],
            at_in + [(a, VMEM) for a in (piece, near, far, swap.along(far, "core"))],
            [],
            3,
            "spread",
        )[0]

    block_out = spread(own_out, out_far)
    grad_keep, grad_send = kernel_call(
        normed_body,
        [share_single, share_half],
        at_in + [(after(attn_full, *before_normed), VMEM)] + [(a, VMEM) for a in grad_qkv],
        [wide],
        5,
        "normed",
    )
    grad_came = swap.along(grad_send, "core")

    small_out = (
        [(shape((n_dp * n_tensor, SMALL_ROWS, 128), HALF), VMEM)]
        if direct
        else [
            (shape((4 * PLACE_ROWS, width), SINGLE), VMEM),
            (shape((n_tensor, 1, 3 * columns), SINGLE), VMEM),
            (shape((n_tensor, 1, hidden), SINGLE), VMEM),
        ]
    )
    end_scratch = [pltpu.VMEM((share * pad, width), SINGLE)]
    if direct:
        end_scratch.append(pltpu.VMEM((4 * PLACE_ROWS, width), SINGLE))
    own_grad, *small_grads = kernel_call(
        functools.partial(end_body, share, patch_count, pad, direct),
        [share_half] + small_out,
        at_in
        + [
            (a, VMEM)
            for a in (after(grad_keep, *before_end, block_out), grad_came, start, grad_middle, mask, table, sums_two, sums_expand, *sums_entry)
        ],
        end_scratch,
        8,
        "end",
    )

    grad_far = swap.along(own_grad, "x")
    patch_grad = spread(own_grad, grad_far)

    sum_up = lambda parts: sum(part.astype(SINGLE) for part in parts)
    if direct:
        reduced = sum_up(reduce_parts).T
        expanded = sum_up(expand_parts)
        attn_parts = swap.reduce_line(*swap.reduce_ends(grad_attn[0], attn_early, attn_side))
        (small,) = small_grads
        small = add(small[:16], swap.along(small[16:], "core"))
        small = small.reshape(2, 2, 4, SMALL_ROWS, 128)
        small = add(small[:, 0], swap.along(small[:, 1], "y"))
        attn = sum_up(after(attn_parts, small))
        small = sum_up([small[:, 0]] + [swap.along(small[:, k], f"z{k}") for k in (1, 2, 3)])
        small = after(small, grad_far)
        pair = small + swap.along(small[::-1], "x")
        other = swap.along(after(pair, patch_grad), "core")
        small = pair[0]
        updated = lambda like: [(shape(like.shape, kind), VMEM) for kind in (SINGLE, SINGLE, SINGLE, HALF)]
        exits = kernel_call(
            exit_body,
            updated(exit_weight),
            [(a, VMEM) for a in (attn[:, 3 * columns :], exit_weight, exit_moment, exit_second)],
            [],
            2,
            "exit",
        )
        tables = kernel_call(
            tables_body,
            updated(position.T) + updated(vectors),
            at_in
            + [(a, VMEM) for a in (pair, other, position.T, position_moment.T, position_second.T, vectors, vectors_moment, vectors_second)],
            [pltpu.VMEM((4, SMALL_ROWS, 128), SINGLE), pltpu.VMEM((4 * PLACE_ROWS, 128), SINGLE)],
            2,
            "tables",
        )
        place_new = [a.T for a in tables[:4]]
        table_new = tables[4:]
        grad_expand_shift = small[PLACE_ROWS : PLACE_ROWS + 1, :rows]
        grad_entry_shift = small[PLACE_ROWS + 1 : PLACE_ROWS + 3, : entry_bias.shape[2]][:, None, :]
    else:
        def total(outs):
            mine = outs[0][0].astype(SINGLE)
            for b in range(1, blocks):
                mine = mine + swap.flip(outs[b][0], "tensor", 2 * b).astype(SINGLE)
            return lax.psum_scatter(mine, "dp", scatter_dimension=0, tiled=True)

        reduced = total([outs[0] for outs in grad_reduce]).T
        expanded = total([outs[0] for outs in grad_expand])
        attn = total([outs[0] for outs in grad_attn])
        spot, entry_part, expand_part = small_grads
        spot = lax.psum(lax.psum_scatter(spot, "dp", scatter_dimension=1, tiled=True), "tensor")
        grad_place = spot[:patch_count]
        grad_table = spot[200:207]
        deal = lambda array, axis: lax.psum_scatter(
            lax.psum_scatter(array, "tensor", scatter_dimension=0, tiled=True)[0],
            "dp",
            scatter_dimension=axis,
            tiled=True,
        )
        grad_expand_shift = deal(expand_part, 1)
        ends = [deal(entry_part[:, :, first : first + columns], 1) for first in (0, 2 * columns)]
        grad_entry_shift = jnp.stack(ends)
        exits = adamw(exit_weight, exit_moment, exit_second, attn[:, 3 * columns :].T, 0.05, 0.05)
        table_new = adamw(vectors, vectors_moment, vectors_second, grad_table, 0.3, 0.0)
        place_new = adamw(position, position_moment, position_second, grad_place, 0.1, 0.0)

    grad_entry = jnp.stack([attn[:, j * columns : (j + 1) * columns] for j in range(3)])

    entry = adamw(entry_weight, entry_moment, entry_second, grad_entry, 0.05, 0.05)
    entry_b = adamw(entry_bias, entry_bias_moment, entry_bias_second, grad_entry_shift, 0.3, 0.0)
    expand = adamw(expand_weight, expand_moment, expand_second, expanded, 0.05, 0.05)
    expand_b = adamw(expand_bias, expand_bias_moment, expand_bias_second, grad_expand_shift, 0.3, 0.0)
    reduce_w = adamw(reduce_weight, reduce_moment, reduce_second, reduced, 0.05, 0.05)
    return (block_out, patch_grad, *entry, *entry_b, *exits, *expand, *expand_b, *reduce_w, *table_new, *place_new)


def solution(mesh):
    images = P("dp", None, None)
    entry = P(None, "dp", "tensor")
    entry_bias = P(None, "tensor", "dp")
    outer = P("tensor", "dp")
    expand = P("dp", "tensor")
    table = P(None, "dp")
    weights = (entry, entry_bias, outer, expand, outer, outer, table, table)
    placed = (images, images, P("dp", None), P("dp"), P("dp"))
    placed += tuple(spec for spec in weights for _ in range(3))
    given = (images, images) + tuple(spec for spec in weights for _ in range(4))
    sizes = (mesh.shape["dp"], mesh.shape["tensor"])
    return jax.shard_map(
        functools.partial(local, sizes),
        mesh=mesh,
        in_specs=placed,
        out_specs=given,
        check_vma=False,
    )
```
